768 devices in a mesh: rows: 384 (over z, x, y), cols: 2 (over core).
Axes of the slice: x: 4, y: 8, z: 12, core: 2. Of those that a mesh axis runs over, the one named last changes fastest.
Arguments:
- start: float32 [147456, 256], P('rows', 'cols'), may hold values from -24 to 24
- tiles: bfloat16 [13824, 128, 128], P('rows'), may hold values from -0.078125 to 0.078125
- tile_cols: int32 [13824], P('rows'), may hold values from 0 to 1151, as said below
Outputs:
- embedding: float32 [147456, 256], P('rows', 'cols')
The draws below stay inside these ranges and needn't reach their ends.
Inputs may be any that keep to these rules, and one draw needn't show every extreme that they name: `tile_cols`: a tile of a block row held by rows index d has its column block from d * 3 - 2 to (d + 1) * 3 + 1.
All inputs are finite; a program needn't handle non-finite values.
Results may differ from the reference program's by a relative error of at most 0.007.
Values may be sent and summed in bfloat16 or wider, within the bound.
A program may use at most 32 MiB of HBM per device.

```python
import jax
import jax.numpy as jnp
from jax import lax

NV = 256
TILE = 128
BR_DEV = 3
TPR = 12
CUT = 2
DEGREE = 3
ITERS = 2
NB = 1152
NODES = 147456
N_ROWS = 384


def draw_start(key, part):
    first, second = jax.random.split(key, 2)
    base = jax.random.normal(first, (NODES, NV), jnp.float32)
    rough = jax.random.uniform(second, (NODES, 1), jnp.float32, 0.5, 1.5)
    ramp = 1.0 + 2.0 * (jnp.arange(NODES) // TILE).astype(jnp.float32) / (NB - 1)
    return jnp.clip(base * rough * ramp[:, None], -24.0, 24.0).astype(jnp.float32)


def draw_tile_cols(key, part):
    total = NB * TPR
    index = jnp.arange(total, dtype=jnp.int32)
    slot = index % TPR
    device = index // TPR // BR_DEV
    lowest = device * BR_DEV - CUT
    span = BR_DEV + 2 * CUT
    picked = jax.random.randint(key, (total,), 0, span, dtype=jnp.int32) + lowest
    picked = jnp.where(slot == 0, lowest, picked)
    picked = jnp.where(slot == 1, lowest + span - 1, picked)
    return jnp.clip(picked, 0, NB - 1).astype(jnp.int32)


def block_levels(own_key, extent, cuts, least, largest):
    loudness, own = 1.0, jax.random.fold_in(own_key, 6)
    for dim, parts in cuts:
        heights = jnp.exp(jax.random.uniform(jax.random.fold_in(own, dim), (parts,), jnp.float32, least / len(cuts), largest / len(cuts)))
        loudness = loudness * jnp.repeat(heights, extent[dim] // parts).reshape([-1 if axis == dim else 1 for axis in range(len(extent))])
    return loudness


def gaussian(rng, dims, width, most, pieces=(), kind=jnp.bfloat16):
    array = jax.random.normal(rng, dims, jnp.float32) * width
    if len(pieces) > 0:
        array = block_levels(rng, dims, pieces, -0.22, 0.18) * array
    return jnp.clip(array, min=-most, max=most).astype(kind)


def setup_inputs(seed: int = 0) -> dict:
    key_of = jax.random.split(jax.random.key(seed), 4)
    return {
        "start": draw_start(jax.random.fold_in(key_of[3], 71), 0),
        "tiles": gaussian(key_of[1], (NB * TPR, TILE, TILE), (4 * TPR * TILE) ** -0.5, 0.078125, ((0, 384),)),
        "tile_cols": draw_tile_cols(jax.random.fold_in(key_of[3], 71), 0),
    }


def apply_adjacency(zmat, tiles, tile_cols):
    blocks = zmat.reshape(NB, TILE, NV)
    tile_groups = tiles.reshape(N_ROWS, BR_DEV, TPR, TILE, TILE)
    col_groups = tile_cols.reshape(N_ROWS, BR_DEV, TPR)

    def one_group(pair):
        group_tiles, group_cols = pair
        selected = blocks[group_cols].astype(jnp.float32)
        return jnp.einsum('rtij,rtjc->ric', group_tiles.astype(jnp.float32), selected)
    result = lax.map(one_group, (tile_groups, col_groups))
    return result.reshape(NODES, NV)

def reference(start, tiles, tile_cols):
    current = start
    for outer in range(ITERS):
        y_prev = current
        product = apply_adjacency(current.astype(jnp.bfloat16), tiles, tile_cols)
        y_curr = ((1.0 - 1.25) * current - product) / 0.75
        for step in range(1, DEGREE):
            product = apply_adjacency(y_curr.astype(jnp.bfloat16), tiles, tile_cols)
            y_next = 2.0 * ((1.0 - 1.25) * y_curr - product) / 0.75 - y_prev
            y_prev = y_curr
            y_curr = y_next
        gram = jnp.dot(y_curr.T.astype(jnp.float32), y_curr.astype(jnp.float32), precision=lax.Precision.HIGHEST, preferred_element_type=jnp.float32) / NODES
        factor = jnp.linalg.cholesky(gram)
        inverse = lax.linalg.triangular_solve(factor, jnp.eye(NV, dtype=gram.dtype), left_side=True, lower=True)
        current = jnp.dot(y_curr.astype(jnp.float32), inverse.T.astype(jnp.float32), precision=lax.Precision.HIGHEST, preferred_element_type=jnp.float32)
    return current
```

```python
import functools

import jax
import jax.numpy as jnp
from jax import lax
from jax.experimental import pallas as pl
from jax.experimental.pallas import tpu as pltpu
from jax.sharding import PartitionSpec as P

TILE = 128
BR = 3
TPR = 12
CUT = 2
SPAN = BR + 2 * CUT
DEGREE = 3
ITERS = 2
OWN = BR * TILE
EXT = SPAN * TILE
LOW = CUT * TILE
AXES = (12, 4, 8)
MESH = pl.DeviceIdType.MESH
VMEM = pl.BlockSpec(memory_space=pltpu.VMEM)
F32 = jnp.float32
BF16 = jnp.bfloat16
HIGHEST = lax.Precision.HIGHEST


def dot(a, b, contract, precision=None):
    return lax.dot_general(
        a, b, (contract, ((), ())), precision=precision, preferred_element_type=F32
    )


def band_kernel(cols_ref, tiles_ref, band_ref):
    lowest = lax.axis_index("rows") * BR - CUT
    for r in range(BR):
        sums = [jnp.zeros((TILE, TILE), F32) for _ in range(SPAN)]
        for t in range(TPR):
            tile = tiles_ref[r * TPR + t].astype(F32)
            place = cols_ref[r * TPR + t] - lowest
            for b in range(SPAN):
                sums[b] = sums[b] + jnp.where(place == b, tile, 0.0)
        for b in range(SPAN):
            high = sums[b].astype(BF16)
            rows = slice(r * TILE, (r + 1) * TILE)
            lanes = slice(b * TILE, (b + 1) * TILE)
            band_ref[0, rows, lanes] = high
            band_ref[1, rows, lanes] = (sums[b] - high.astype(F32)).astype(BF16)


def build_band(tiles, tile_cols):
    return pl.pallas_call(
        band_kernel,
        out_shape=jax.ShapeDtypeStruct((2, OWN, EXT), BF16),
        in_specs=[pl.BlockSpec(memory_space=pltpu.SMEM), VMEM],
        out_specs=VMEM,
        name="band",
    )(tile_cols, tiles)


def filter_kernel(
    axes, x_ref, band_ref, full_ref, gram_ref,
    z, y1, part, rx, s1, ry, rz,
    halo_s, halo_r, pair_s, pair_r, x_s, x_r, y_s, y_r, z_s, z_r, gy_s, gy_r, gx_s, gx_r, gc_s, gc_r,
):
    NZ, NX, NY = axes
    T = 32 // (NX * NY)
    me = lax.axis_index("rows")
    core = lax.axis_index("cols")
    my_z, my_x, my_y = me // (NX * NY), (me // NY) % NX, me % NY
    count = NZ * NX * NY

    def row(zz, xx, yy):
        return (zz * NX + xx) * NY + yy

    right, left = lax.rem(me + 1, count), lax.rem(me + count - 1, count)
    to_x = [row(my_z, lax.rem(my_x + d, NX), my_y) for d in range(NX)]
    to_y = [row(my_z, my_x, lax.rem(my_y + d, NY)) for d in range(NY)]
    to_z = [row(lax.rem(my_z + d, NZ), my_x, my_y) for d in range(NZ)]

    barrier = pltpu.get_barrier_semaphore()
    greet = [(left, core), (right, core), (me, 1 - core)]
    greet += [(r, core) for r in to_x[1:] + to_y[1:] + to_z[1:]]
    greet += [(r, 1 - core) for r in to_x[1:]]
    for device in greet:
        pl.semaphore_signal(barrier, inc=1, device_id=device, device_id_type=MESH)
    pl.semaphore_wait(barrier, len(greet))

    def remote(src, dst, send, recv, device):
        return pltpu.make_async_remote_copy(
            src_ref=src, dst_ref=dst, send_sem=send, recv_sem=recv,
            device_id=device, device_id_type=MESH,
        )

    sent = []

    def start(copy):
        copy.start()
        sent.append(copy)

    def band_dot(lanes, values):
        return dot(band_ref[0, :, lanes], values, ((1,), (0,))) + dot(
            band_ref[1, :, lanes], values, ((1,), (0,))
        )

    own = slice(LOW, LOW + OWN)
    y_prev = None
    for step in range(DEGREE):
        current = x_ref if step == 0 else y1 if step == 1 else part
        y_curr = current[...]
        z[step, own, :] = y_curr.astype(BF16)
        down = remote(
            z.at[step, pl.ds(LOW, LOW)], z.at[step, pl.ds(LOW + OWN, LOW)],
            halo_s.at[step, 0], halo_r.at[step, 0], (left, core),
        )
        up = remote(
            z.at[step, pl.ds(OWN, LOW)], z.at[step, pl.ds(0, LOW)],
            halo_s.at[step, 1], halo_r.at[step, 1], (right, core),
        )
        start(down)
        start(up)
        product = band_dot(own, z[step, own, :])
        up.wait_recv()
        product += band_dot(slice(0, LOW), z[step, 0:LOW, :])
        down.wait_recv()
        product += band_dot(slice(LOW + OWN, EXT), z[step, LOW + OWN : EXT, :])
        if step == 0:
            y1[...] = ((1.0 - 1.25) * y_curr - product) / 0.75
        elif step == 1:
            part[...] = 2.0 * ((1.0 - 1.25) * y_curr - product) / 0.75 - x_ref[...]
        else:
            full_ref[core] = 2.0 * ((1.0 - 1.25) * y_curr - product) / 0.75 - y1[...]

    pair = remote(full_ref.at[core], full_ref.at[core], pair_s, pair_r, (me, 1 - core))
    start(pair)
    pair.wait_recv()
    mine = full_ref[core]
    local = s1
    for half in range(2):
        block = dot(full_ref[half], mine, ((0,), (0,)), HIGHEST)
        for t in range(16):
            tile = half * 16 + t
            k, xx, yy = tile % T, tile // T % NX, tile // (T * NX)
            local[xx, yy, k] = block[8 * t : 8 * t + 8, :]

    for d in range(1, NX):
        start(remote(local.at[lax.rem(my_x + d, NX)], rx.at[d], x_s.at[d], x_r.at[d], (to_x[d], core)))
    rx[0] = local[my_x]
    for d in range(1, NX):
        remote(local.at[0], rx.at[d], x_s.at[d], x_r.at[d], (to_x[d], core)).wait_recv()
    total = rx[0]
    for d in range(1, NX):
        total += rx[d]
    rx[0] = total
    for d in range(1, NY):
        start(remote(rx.at[0, lax.rem(my_y + d, NY)], ry.at[d], y_s.at[d], y_r.at[d], (to_y[d], core)))
    ry[0] = rx[0, my_y]
    for d in range(1, NY):
        remote(rx.at[0, 0], ry.at[d], y_s.at[d], y_r.at[d], (to_y[d], core)).wait_recv()
    total = ry[0]
    for d in range(1, NY):
        total += ry[d]
    rz[my_z] = total
    for d in range(1, NZ):
        start(remote(rz.at[my_z], rz.at[my_z], z_s.at[d], z_r.at[d], (to_z[d], core)))
    for d in range(1, NZ):
        remote(rz.at[0], rz.at[0], z_s.at[d], z_r.at[d], (to_z[d], core)).wait_recv()
    total = rz[0]
    for d in range(1, NZ):
        total += rz[d]
    gram_ref[core, my_x, my_y] = total / (count * OWN)
    for d in range(1, NY):
        chunk = gram_ref.at[core, my_x, my_y]
        start(remote(chunk, chunk, gy_s.at[d], gy_r.at[d], (to_y[d], core)))
    for d in range(1, NY):
        chunk = gram_ref.at[0, 0, 0]
        remote(chunk, chunk, gy_s.at[d], gy_r.at[d], (to_y[d], core)).wait_recv()
    slab = gram_ref.at[core, my_x]
    for d in range(1, NX):
        start(remote(slab, slab, gx_s.at[d], gx_r.at[d], (to_x[d], core)))

    def cross(d):
        return remote(slab, slab, gc_s.at[d], gc_r.at[d], (to_x[d], 1))

    @pl.when(core == 0)
    def _():
        for d in range(NX):
            cross(d).start()

    for d in range(1, NX):
        remote(slab, slab, gx_s.at[d], gx_r.at[d], (to_x[d], core)).wait_recv()

    @pl.when(core == 1)
    def _():
        for d in range(NX):
            remote(slab, slab, gc_s.at[d], gc_r.at[d], (me, 0)).wait_recv()

    @pl.when(core == 0)
    def _():
        for d in range(NX):
            cross(d).wait_send()

    for copy in sent:
        copy.wait_send()


def filter_and_gram(axes, x, band):
    NZ, NX, NY = axes
    T = 32 // (NX * NY)
    dma = pltpu.SemaphoreType.DMA
    return pl.pallas_call(
        functools.partial(filter_kernel, axes),
        out_shape=(
            jax.ShapeDtypeStruct((2, OWN, TILE), F32),
            jax.ShapeDtypeStruct((2, NX, NY, T, 8, TILE), F32),
        ),
        in_specs=[VMEM, VMEM],
        out_specs=(VMEM, VMEM),
        scratch_shapes=[
            pltpu.VMEM((DEGREE, EXT, TILE), BF16),
            pltpu.VMEM((OWN, TILE), F32),
            pltpu.VMEM((OWN, TILE), F32),
            pltpu.VMEM((NX, NY, T, 8, TILE), F32),
            pltpu.VMEM((NX, NY, T, 8, TILE), F32),
            pltpu.VMEM((NY, T, 8, TILE), F32),
            pltpu.VMEM((NZ, T, 8, TILE), F32),
            dma((DEGREE, 2)), dma((DEGREE, 2)), dma, dma,
            dma((NX,)), dma((NX,)), dma((NY,)), dma((NY,)), dma((NZ,)), dma((NZ,)),
            dma((NY,)), dma((NY,)), dma((NX,)), dma((NX,)), dma((NX,)), dma((NX,)),
        ],
        compiler_params=pltpu.CompilerParams(collective_id=0, has_side_effects=True),
        name="filter",
    )(x, band)


def lane_copy(v, c):
    return jnp.broadcast_to(v[:, c : c + 1], (8, TILE))


def row_copy(v, r):
    return jnp.broadcast_to(v[r : r + 1, :], (8, TILE))


def inverse_factor(m):
    lane = lax.broadcasted_iota(jnp.int32, (8, TILE), 1)
    sub = lax.broadcasted_iota(jnp.int32, (8, TILE), 0)
    m = list(m)
    w = [None] * 16
    for g in range(16):
        first = 8 * g
        spread = [lane_copy(m[g], first + k) for k in range(8)]
        a = [[row_copy(spread[k], i) if i >= k else None for k in range(8)] for i in range(8)]
        inside = (lane >= first) & (lane < first + 8)
        rows = jnp.where(inside, jnp.where(lane == sub + first, 1.0, 0.0), m[g])
        r = [None] * 8
        c = [[None] * 8 for _ in range(8)]
        for k in range(8):
            r[k] = lax.rsqrt(a[k][k])
            for i in range(k + 1, 8):
                c[i][k] = a[i][k] * r[k]
            for j in range(k + 1, 8):
                for i in range(j, 8):
                    a[i][j] = a[i][j] - c[i][k] * c[j][k]
        solved = [row_copy(rows, k) for k in range(8)]
        for k in range(8):
            solved[k] = solved[k] * r[k]
            for j in range(k + 1, 8):
                solved[j] = solved[j] - c[j][k] * solved[k]
        group = solved[0]
        for k in range(1, 8):
            group = jnp.where(sub == k, solved[k], group)
        w[g] = jnp.where(lane < first + 8, group, 0.0)
        for i in range(g + 1, 16):
            p = [lane_copy(m[i], first + k) for k in range(8)]
            rest = jnp.where(inside, 0.0, m[i])
            for k in range(8):
                col = p[k] * r[k]
                for j in range(k + 1, 8):
                    p[j] = p[j] - c[j][k] * col
                rest = rest - col * solved[k]
            m[i] = rest
    return w


def update_kernel(axes, full_ref, gram_ref, out_ref, gaa, gba, gbb, waa, wbb):
    NZ, NX, NY = axes
    T = 32 // (NX * NY)
    core = lax.axis_index("cols")
    for t in range(16):
        for half, panel, dst in ((0, 0, gaa), (1, 0, gba), (1, 1, gbb)):
            tile = half * 16 + t
            k, xx, yy = tile % T, tile // T % NX, tile // (T * NX)
            dst[8 * t : 8 * t + 8, :] = gram_ref[panel, xx, yy, k]
    for t, group in enumerate(inverse_factor([gaa[8 * i : 8 * i + 8, :] for i in range(16)])):
        waa[8 * t : 8 * t + 8, :] = group

    @pl.when(core == 0)
    def _():
        out_ref[...] = dot(full_ref[0], waa[...], ((1,), (1,)), HIGHEST)

    @pl.when(core == 1)
    def _():
        cba = dot(gba[...], waa[...], ((1,), (1,)), HIGHEST)
        gbb[...] = gbb[...] - dot(cba, cba, ((1,), (1,)), HIGHEST)
        shift = dot(cba, waa[...], ((1,), (0,)), HIGHEST)
        rest = full_ref[1] - dot(full_ref[0], shift, ((1,), (1,)), HIGHEST)
        for t, group in enumerate(inverse_factor([gbb[8 * i : 8 * i + 8, :] for i in range(16)])):
            wbb[8 * t : 8 * t + 8, :] = group
        out_ref[...] = dot(rest, wbb[...], ((1,), (1,)), HIGHEST)


def orthogonalize(axes, full, gram):
    square = pltpu.VMEM((TILE, TILE), F32)
    return pl.pallas_call(
        functools.partial(update_kernel, axes),
        out_shape=jax.ShapeDtypeStruct((OWN, TILE), F32),
        in_specs=[VMEM, VMEM],
        out_specs=VMEM,
        scratch_shapes=[square] * 5,
        name="orthogonalize",
    )(full, gram)


def per_device(axes, start, tiles, tile_cols):
    band = build_band(tiles, tile_cols)
    x = start
    for _ in range(ITERS):
        full, gram = filter_and_gram(axes, x, band)
        x = orthogonalize(axes, full, gram)
    return x


def solution(mesh, axes=AXES):
    placed = (P("rows", "cols"), P("rows", None, None), P("rows"))
    return jax.shard_map(
        functools.partial(per_device, axes),
        mesh=mesh, in_specs=placed, out_specs=P("rows", "cols"), check_vma=False,
    )
```

```python
import functools

import jax
import jax.numpy as jnp
from jax import lax
from jax.experimental import pallas as pl
from jax.experimental.pallas import tpu as pltpu
from jax.sharding import PartitionSpec as P

TILE = 128
BR = 3
TPR = 12
CUT = 2
SPAN = BR + 2 * CUT
DEGREE = 3
ITERS = 2
OWN = BR * TILE
EXT = SPAN * TILE
LOW = CUT * TILE
AXES = (12, 4, 8)
MESH = pl.DeviceIdType.MESH
ANY = pl.BlockSpec(memory_space=pl.ANY)
F32 = jnp.float32
BF16 = jnp.bfloat16
HIGHEST = lax.Precision.HIGHEST


def dot(a, b, contract, precision=None):
    return lax.dot_general(
        a, b, (contract, ((), ())), precision=precision, preferred_element_type=F32
    )


def lane_copy(v, c):
    return jnp.broadcast_to(v[:, c : c + 1], (8, TILE))


def row_copy(v, r):
    return jnp.broadcast_to(v[r : r + 1, :], (8, TILE))


def inverse_factor(m):
    lane = lax.broadcasted_iota(jnp.int32, (8, TILE), 1)
    sub = lax.broadcasted_iota(jnp.int32, (8, TILE), 0)
    m = list(m)
    w = [None] * 16
    for g in range(16):
        first = 8 * g
        spread = [lane_copy(m[g], first + k) for k in range(8)]
        a = [[row_copy(spread[k], i) if i >= k else None for k in range(8)] for i in range(8)]
        inside = (lane >= first) & (lane < first + 8)
        rows = jnp.where(inside, jnp.where(lane == sub + first, 1.0, 0.0), m[g])
        r = [None] * 8
        c = [[None] * 8 for _ in range(8)]
        for k in range(8):
            r[k] = lax.rsqrt(a[k][k])
            for i in range(k + 1, 8):
                c[i][k] = a[i][k] * r[k]
            for j in range(k + 1, 8):
                for i in range(j, 8):
                    a[i][j] = a[i][j] - c[i][k] * c[j][k]
        solved = [row_copy(rows, k) for k in range(8)]
        for k in range(8):
            solved[k] = solved[k] * r[k]
            for j in range(k + 1, 8):
                solved[j] = solved[j] - c[j][k] * solved[k]
        group = solved[0]
        for k in range(1, 8):
            group = jnp.where(sub == k, solved[k], group)
        w[g] = jnp.where(lane < first + 8, group, 0.0)
        for i in range(g + 1, 16):
            p = [lane_copy(m[i], first + k) for k in range(8)]
            rest = jnp.where(inside, 0.0, m[i])
            for k in range(8):
                col = p[k] * r[k]
                for j in range(k + 1, 8):
                    p[j] = p[j] - c[j][k] * col
                rest = rest - col * solved[k]
            m[i] = rest
    return w


def kernel(
    axes, cols_ref, x_ref, tiles_ref, out_ref,
    tiles, band, x, z, y1, y2, y3, other, m, w, waa,
    part_a, part_b, plane_a, plane_b, line_a, line_b, gram_a, gram_b,
    load, halo_s, halo_r, pair_s, pair_r, plane_s, plane_r, line_s, line_r, gram_s, gram_r,
):
    NZ, NX, NY = axes
    NQ = NX * NY
    me = lax.axis_index("rows")
    core = lax.axis_index("cols")
    my_z, my_q = me // NQ, me % NQ
    my_x, my_y = my_q // NY, my_q % NY
    count = NZ * NQ
    right, left = lax.rem(me + 1, count), lax.rem(me + count - 1, count)
    in_plane = [
        lax.rem(my_x + dx, NX) * NY + lax.rem(my_y + dy, NY)
        for dx in range(NX) for dy in range(NY) if dx or dy
    ]
    in_line = [lax.rem(my_z + d, NZ) for d in range(1, NZ)]

    barrier = pltpu.get_barrier_semaphore()
    greet = [(left, core), (right, core), (me, 1 - core)]
    greet += [(my_z * NQ + q, core) for q in in_plane]
    greet += [(zz * NQ + my_q, core) for zz in in_line]
    for device in greet:
        pl.semaphore_signal(barrier, inc=1, device_id=device, device_id_type=MESH)
    load_x = pltpu.make_async_copy(x_ref, x, load.at[0])
    load_tiles = pltpu.make_async_copy(tiles_ref, tiles, load.at[1])
    load_x.start()
    load_tiles.start()
    load_x.wait()
    z[0, LOW : LOW + OWN, :] = x[...].astype(BF16)
    pl.semaphore_wait(barrier, len(greet))

    def remote(src, dst, send, recv, device):
        return pltpu.make_async_remote_copy(
            src_ref=src, dst_ref=dst, send_sem=send, recv_sem=recv,
            device_id=device, device_id_type=MESH,
        )

    def halo(s):
        down = remote(
            z.at[s, pl.ds(LOW, LOW)], z.at[s, pl.ds(LOW + OWN, LOW)],
            halo_s.at[s, 0], halo_r.at[s, 0], (left, core),
        )
        up = remote(
            z.at[s, pl.ds(OWN, LOW)], z.at[s, pl.ds(0, LOW)],
            halo_s.at[s, 1], halo_r.at[s, 1], (right, core),
        )
        return down, up

    def begin_halo(s):
        for copy in halo(s):
            copy.start()

    def band_dot(lanes, values):
        return dot(band[0, :, lanes], values, ((1,), (0,))) + dot(
            band[1, :, lanes], values, ((1,), (0,))
        )

    def apply(s):
        down, up = halo(s)
        product = band_dot(slice(LOW, LOW + OWN), z[s, LOW : LOW + OWN, :])
        up.wait_recv()
        product += band_dot(slice(0, LOW), z[s, 0:LOW, :])
        down.wait_recv()
        product += band_dot(slice(LOW + OWN, EXT), z[s, LOW + OWN : EXT, :])
        return product

    def send_on(s, value):
        z[s, LOW : LOW + OWN, :] = value.astype(BF16)
        begin_halo(s)

    begin_halo(0)
    load_tiles.wait()
    lowest = me * BR - CUT
    for r in range(BR):
        sums = [jnp.zeros((TILE, TILE), F32) for _ in range(SPAN)]
        for t in range(TPR):
            tile = tiles[r * TPR + t].astype(F32)
            place = cols_ref[r * TPR + t] - lowest
            for b in range(SPAN):
                sums[b] = sums[b] + jnp.where(place == b, tile, 0.0)
        for b in range(SPAN):
            high = sums[b].astype(BF16)
            rows = slice(r * TILE, (r + 1) * TILE)
            lanes = slice(b * TILE, (b + 1) * TILE)
            band[0, rows, lanes] = high
            band[1, rows, lanes] = (sums[b] - high.astype(F32)).astype(BF16)

    def sum_over_rows(it, part, plane, line, gram):
        for i, q in enumerate(in_plane):
            remote(
                part.at[it, q], plane.at[it, i + 1], plane_s.at[it], plane_r.at[it], (my_z * NQ + q, core)
            ).start()
        total = part[it, my_q]
        rest = pl.ds(1, NQ - 1)
        all_of_plane = remote(plane.at[it, rest], plane.at[it, rest], plane_s.at[it], plane_r.at[it], (me, 1 - core))
        all_of_plane.wait_recv()
        for i in range(1, NQ):
            total += plane[it, i]
        line[it, my_z] = total
        mine = line.at[it, my_z]
        for zz in in_line:
            remote(mine, mine, line_s.at[it], line_r.at[it], (zz * NQ + my_q, core)).start()
        rest = pl.ds(0, NZ - 1)
        all_of_line = remote(line.at[it, rest], line.at[it, rest], line_s.at[it], line_r.at[it], (me, 1 - core))
        all_of_line.wait_recv()
        total = line[it, 0]
        for i in range(1, NZ):
            total += line[it, i]
        gram[it, my_q] = total / (count * OWN)
        mine = gram.at[it, my_q]
        for q in in_plane:
            remote(mine, mine, gram_s.at[it], gram_r.at[it], (my_z * NQ + q, core)).start()
        rest = pl.ds(0, NQ - 1)
        all_of_gram = remote(gram.at[it, rest], gram.at[it, rest], gram_s.at[it], gram_r.at[it], (me, 1 - core))
        all_of_gram.wait_recv()
        for copy in (all_of_plane, all_of_line, all_of_gram):
            copy.wait_send()

    def iteration(it, carry):
        first = it * DEGREE

        @pl.when(it > 0)
        def _():
            send_on(first, x[...])

        y1[...] = ((1.0 - 1.25) * x[...] - apply(first)) / 0.75
        send_on(first + 1, y1[...])
        y2[...] = 2.0 * ((1.0 - 1.25) * y1[...] - apply(first + 1)) / 0.75 - x[...]
        send_on(first + 2, y2[...])
        y3[it] = 2.0 * ((1.0 - 1.25) * y2[...] - apply(first + 2)) / 0.75 - y1[...]
        give_y = remote(y3.at[it], other.at[it], pair_s.at[it, 0], pair_r.at[it, 0], (me, 1))
        give_w = remote(w.at[it], waa.at[it], pair_s.at[it, 1], pair_r.at[it, 1], (me, 1))
        take_y = remote(y3.at[it], other.at[it], pair_s.at[it, 0], pair_r.at[it, 0], (me, 0))
        take_w = remote(w.at[it], waa.at[it], pair_s.at[it, 1], pair_r.at[it, 1], (me, 0))
        rows_a, rows_b = TILE // NQ, 2 * TILE // NQ

        @pl.when(core == 0)
        def _():
            give_y.start()
            y = y3[it]
            block = dot(y, y, ((0,), (0,)), HIGHEST)
            for q in range(NQ):
                part_a[it, q] = block[rows_a * q : rows_a * (q + 1), :]
            sum_over_rows(it, part_a, plane_a, line_a, gram_a)
            for q in range(NQ):
                m[rows_a * q : rows_a * (q + 1), :] = gram_a[it, q]

        @pl.when(core == 1)
        def _():
            y = y3[it]
            block = dot(y, y, ((0,), (0,)), HIGHEST)
            for q in range(NQ // 2):
                part_b[it, NQ // 2 + q] = block[rows_b * q : rows_b * (q + 1), :]
            take_y.wait_recv()
            block = dot(other[it], y, ((0,), (0,)), HIGHEST)
            for q in range(NQ // 2):
                part_b[it, q] = block[rows_b * q : rows_b * (q + 1), :]
            sum_over_rows(it, part_b, plane_b, line_b, gram_b)
            take_w.wait_recv()
            gab = gram_b[it, 0 : NQ // 2].reshape(TILE, TILE)
            gbb = gram_b[it, NQ // 2 :].reshape(TILE, TILE)
            cab = dot(waa[it], gab, ((1,), (0,)), HIGHEST)
            m[...] = gbb - dot(cab, cab, ((0,), (0,)), HIGHEST)
            shift = dot(waa[it], cab, ((0,), (0,)), HIGHEST)
            y3[it] = y - dot(other[it], shift, ((1,), (0,)), HIGHEST)

        for g, group in enumerate(inverse_factor([m[8 * i : 8 * i + 8, :] for i in range(16)])):
            w[it, 8 * g : 8 * g + 8, :] = group

        @pl.when(core == 0)
        def _():
            give_w.start()

        x[...] = dot(y3[it], w[it], ((1,), (1,)), HIGHEST)

        @pl.when(core == 0)
        def _():
            give_y.wait_send()
            give_w.wait_send()

        for step in range(DEGREE):
            for copy in halo(first + step):
                copy.wait_send()
        return carry

    lax.fori_loop(0, ITERS, iteration, 0)
    out_ref[...] = x[...]


def per_device(axes, start, tiles, tile_cols):
    NZ, NX, NY = axes
    NQ = NX * NY
    rows_a, rows_b = TILE // NQ, 2 * TILE // NQ
    dma = pltpu.SemaphoreType.DMA
    steps = ITERS * DEGREE

    def vmem(*shape, dtype=F32):
        return pltpu.VMEM(shape, dtype)

    return pl.pallas_call(
        functools.partial(kernel, axes),
        out_shape=jax.ShapeDtypeStruct((OWN, TILE), F32),
        in_specs=[pl.BlockSpec(memory_space=pltpu.SMEM), ANY, ANY],
        out_specs=pl.BlockSpec(memory_space=pltpu.VMEM),
        scratch_shapes=[
            vmem(BR * TPR, TILE, TILE, dtype=BF16),
            vmem(2, OWN, EXT, dtype=BF16),
            vmem(OWN, TILE),
            vmem(steps, EXT, TILE, dtype=BF16),
            vmem(OWN, TILE), vmem(OWN, TILE), vmem(ITERS, OWN, TILE), vmem(ITERS, OWN, TILE),
            vmem(TILE, TILE), vmem(ITERS, TILE, TILE), vmem(ITERS, TILE, TILE),
            vmem(ITERS, NQ, rows_a, TILE), vmem(ITERS, NQ, rows_b, TILE),
            vmem(ITERS, NQ, rows_a, TILE), vmem(ITERS, NQ, rows_b, TILE),
            vmem(ITERS, NZ, rows_a, TILE), vmem(ITERS, NZ, rows_b, TILE),
            vmem(ITERS, NQ, rows_a, TILE), vmem(ITERS, NQ, rows_b, TILE),
            dma((2,)), dma((steps, 2)), dma((steps, 2)), dma((ITERS, 2)), dma((ITERS, 2)),
        ] + [dma((ITERS,))] * 6,
        compiler_params=pltpu.CompilerParams(collective_id=0, has_side_effects=True),
        name="embed",
    )(tile_cols, start, tiles)


def solution(mesh, axes=AXES):
    placed = (P("rows", "cols"), P("rows", None, None), P("rows"))
    return jax.shard_map(
        functools.partial(per_device, axes),
        mesh=mesh, in_specs=placed, out_specs=P("rows", "cols"), check_vma=False,
    )
```

```python
import functools

import jax
import jax.numpy as jnp
from jax import lax
from jax.experimental import pallas as pl
from jax.experimental.pallas import tpu as pltpu
from jax.sharding import PartitionSpec as P

TILE = 128
BR = 3
TPR = 12
CUT = 2
SPAN = BR + 2 * CUT
DEGREE = 3
ITERS = 2
OWN = BR * TILE
EXT = SPAN * TILE
LOW = CUT * TILE
AXES = (12, 4, 8)
MESH = pl.DeviceIdType.MESH
ANY = pl.BlockSpec(memory_space=pl.ANY)
F32 = jnp.float32
BF16 = jnp.bfloat16
HIGHEST = lax.Precision.HIGHEST


def dot(a, b, contract, precision=None):
    return lax.dot_general(
        a, b, (contract, ((), ())), precision=precision, preferred_element_type=F32
    )


def lane_copy(v, c):
    return jnp.broadcast_to(v[:, c : c + 1], (8, TILE))


def row_copy(v, r):
    return jnp.broadcast_to(v[r : r + 1, :], (8, TILE))


def inverse_factor(m):
    lane = lax.broadcasted_iota(jnp.int32, (8, TILE), 1)
    sub = lax.broadcasted_iota(jnp.int32, (8, TILE), 0)
    m = list(m)
    w = [None] * 16
    for g in range(16):
        first = 8 * g
        spread = [lane_copy(m[g], first + k) for k in range(8)]
        a = [[row_copy(spread[k], i) if i >= k else None for k in range(8)] for i in range(8)]
        inside = (lane >= first) & (lane < first + 8)
        rows = jnp.where(inside, jnp.where(lane == sub + first, 1.0, 0.0), m[g])
        r = [None] * 8
        c = [[None] * 8 for _ in range(8)]
        for k in range(8):
            r[k] = lax.rsqrt(a[k][k])
            for i in range(k + 1, 8):
                c[i][k] = a[i][k] * r[k]
            for j in range(k + 1, 8):
                for i in range(j, 8):
                    a[i][j] = a[i][j] - c[i][k] * c[j][k]
        solved = [row_copy(rows, k) for k in range(8)]
        for k in range(8):
            solved[k] = solved[k] * r[k]
            for j in range(k + 1, 8):
                solved[j] = solved[j] - c[j][k] * solved[k]
        group = solved[0]
        for k in range(1, 8):
            group = jnp.where(sub == k, solved[k], group)
        w[g] = jnp.where(lane < first + 8, group, 0.0)
        for i in range(g + 1, 16):
            p = [lane_copy(m[i], first + k) for k in range(8)]
            rest = jnp.where(inside, 0.0, m[i])
            for k in range(8):
                col = p[k] * r[k]
                for j in range(k + 1, 8):
                    p[j] = p[j] - c[j][k] * col
                rest = rest - col * solved[k]
            m[i] = rest
    return w


def kernel(
    axes, cols_ref, x_ref, tiles_ref, out_ref,
    tiles, band, x, z, y1, y2, y3, other, m, w, waa, shift, wba,
    part_a, part_b, plane_a, plane_b, line_a, line_b, gram_a, gram_b,
    load, halo_s, halo_r, pair_s, pair_r, edge_s, edge_r, pass_s, pass_r, plane_s, plane_r, line_s, line_r, gram_s, gram_r,
):
    NZ, NX, NY = axes
    NQ = NX * NY
    me = lax.axis_index("rows")
    core = lax.axis_index("cols")
    my_z, my_q = me // NQ, me % NQ
    my_x, my_y = my_q // NY, my_q % NY
    count = NZ * NQ
    right, left = lax.rem(me + 1, count), lax.rem(me + count - 1, count)
    steps = [(dx, dy) for dx in range(NX) for dy in range(NY) if dx or dy]
    steps.sort(key=lambda s: -min(s[0], NX - s[0]) - min(s[1], NY - s[1]))
    in_plane = [lax.rem(my_x + dx, NX) * NY + lax.rem(my_y + dy, NY) for dx, dy in steps]
    in_line = [lax.rem(my_z + d, NZ) for d in sorted(range(1, NZ), key=lambda d: -min(d, NZ - d))]
    load_x = pltpu.make_async_copy(x_ref, x, load.at[0])
    load_tiles = pltpu.make_async_copy(tiles_ref, tiles, load.at[1])
    load_x.start()
    load_tiles.start()

    barrier = pltpu.get_barrier_semaphore()
    greet = [(left, core), (right, core), (me, 1 - core)]
    greet += [(my_z * NQ + q, core) for q in in_plane]
    greet += [(zz * NQ + my_q, core) for zz in in_line]
    for device in greet:
        pl.semaphore_signal(barrier, inc=1, device_id=device, device_id_type=MESH)
    load_x.wait()
    z[0, LOW : LOW + OWN, :] = x[...].astype(BF16)
    pl.semaphore_wait(barrier, len(greet))

    def remote(src, dst, send, recv, device):
        return pltpu.make_async_remote_copy(
            src_ref=src, dst_ref=dst, send_sem=send, recv_sem=recv,
            device_id=device, device_id_type=MESH,
        )

    def edges():
        down = remote(
            y3.at[0, pl.ds(LOW, LOW)], y3.at[0, pl.ds(LOW + OWN, LOW)], edge_s.at[0], edge_r.at[0], (left, core)
        )
        up = remote(y3.at[0, pl.ds(OWN, LOW)], y3.at[0, pl.ds(0, LOW)], edge_s.at[1], edge_r.at[1], (right, core))
        return down, up

    def passes(device):
        return [
            remote(y3.at[0, rows], other.at[0, rows], pass_s.at[i], pass_r.at[i], device)
            for i, rows in enumerate((pl.ds(0, LOW), pl.ds(LOW + OWN, LOW)))
        ]

    def halo(s):
        down = remote(
            z.at[s, pl.ds(LOW, LOW)], z.at[s, pl.ds(LOW + OWN, LOW)],
            halo_s.at[s, 0], halo_r.at[s, 0], (left, core),
        )
        up = remote(
            z.at[s, pl.ds(OWN, LOW)], z.at[s, pl.ds(0, LOW)],
            halo_s.at[s, 1], halo_r.at[s, 1], (right, core),
        )
        return down, up

    def begin_halo(s):
        for copy in halo(s):
            copy.start()

    def band_dot(lanes, values):
        return dot(band[0, :, lanes], values, ((1,), (0,))) + dot(
            band[1, :, lanes], values, ((1,), (0,))
        )

    def apply(s, travelled=True):
        down, up = halo(s)
        product = band_dot(slice(LOW, LOW + OWN), z[s, LOW : LOW + OWN, :])
        pl.when(travelled)(up.wait_recv)
        product += band_dot(slice(0, LOW), z[s, 0:LOW, :])
        pl.when(travelled)(down.wait_recv)
        product += band_dot(slice(LOW + OWN, EXT), z[s, LOW + OWN : EXT, :])
        return product

    def send_on(s, value):
        z[s, LOW : LOW + OWN, :] = value.astype(BF16)
        begin_halo(s)

    begin_halo(0)
    load_tiles.wait()
    lowest = me * BR - CUT
    for r in range(BR):
        sums = [jnp.zeros((TILE, TILE), F32) for _ in range(SPAN)]
        for t in range(TPR):
            tile = tiles[r * TPR + t].astype(F32)
            place = cols_ref[r * TPR + t] - lowest
            for b in range(SPAN):
                sums[b] = sums[b] + jnp.where(place == b, tile, 0.0)
        for b in range(SPAN):
            high = sums[b].astype(BF16)
            rows = slice(r * TILE, (r + 1) * TILE)
            lanes = slice(b * TILE, (b + 1) * TILE)
            band[0, rows, lanes] = high
            band[1, rows, lanes] = (sums[b] - high.astype(F32)).astype(BF16)

    def sum_over_rows(it, part, plane, line, gram):
        for i, q in enumerate(in_plane):
            remote(
                part.at[it, q], plane.at[it, i + 1], plane_s.at[it], plane_r.at[it], (my_z * NQ + q, core)
            ).start()
        total = part[it, my_q]
        rest = pl.ds(1, NQ - 1)
        all_of_plane = remote(plane.at[it, rest], plane.at[it, rest], plane_s.at[it], plane_r.at[it], (me, 1 - core))
        all_of_plane.wait_recv()
        for i in range(1, NQ):
            total += plane[it, i]
        line[it, my_z] = total
        mine = line.at[it, my_z]
        for zz in in_line:
            remote(mine, mine, line_s.at[it], line_r.at[it], (zz * NQ + my_q, core)).start()

        @pl.when(it == 0)
        def _():
            for copy in edges():
                copy.start()

        rest = pl.ds(0, NZ - 1)
        all_of_line = remote(line.at[it, rest], line.at[it, rest], line_s.at[it], line_r.at[it], (me, 1 - core))
        all_of_line.wait_recv()
        total = line[it, 0]
        for i in range(1, NZ):
            total += line[it, i]
        gram[it, my_q] = total / (count * OWN)
        mine = gram.at[it, my_q]
        for q in in_plane:
            remote(mine, mine, gram_s.at[it], gram_r.at[it], (my_z * NQ + q, core)).start()
        rest = pl.ds(0, NQ - 1)
        all_of_gram = remote(gram.at[it, rest], gram.at[it, rest], gram_s.at[it], gram_r.at[it], (me, 1 - core))
        all_of_gram.wait_recv()
        for copy in (all_of_plane, all_of_line, all_of_gram):
            copy.wait_send()

    def iteration(it, carry):
        first = it * DEGREE

        own = slice(LOW, LOW + OWN)
        y1[...] = ((1.0 - 1.25) * x[...] - apply(first, it == 0)) / 0.75
        send_on(first + 1, y1[...])
        y2[...] = 2.0 * ((1.0 - 1.25) * y1[...] - apply(first + 1)) / 0.75 - x[...]
        send_on(first + 2, y2[...])
        y3[it, own, :] = 2.0 * ((1.0 - 1.25) * y2[...] - apply(first + 2)) / 0.75 - y1[...]
        give_y = remote(y3.at[it, pl.ds(LOW, OWN)], other.at[it, pl.ds(LOW, OWN)], pair_s.at[it, 0], pair_r.at[it, 0], (me, 1))
        give_w = remote(w.at[it], waa.at[it], pair_s.at[it, 1], pair_r.at[it, 1], (me, 1))
        take_y = remote(y3.at[it, pl.ds(LOW, OWN)], other.at[it, pl.ds(LOW, OWN)], pair_s.at[it, 0], pair_r.at[it, 0], (me, 0))
        take_w = remote(w.at[it], waa.at[it], pair_s.at[it, 1], pair_r.at[it, 1], (me, 0))
        rows_a, rows_b = TILE // NQ, 2 * TILE // NQ

        @pl.when(core == 0)
        def _():
            give_y.start()
            y = y3[it, own, :]
            block = dot(y, y, ((0,), (0,)), HIGHEST)
            for q in range(NQ):
                part_a[it, q] = block[rows_a * q : rows_a * (q + 1), :]
            sum_over_rows(it, part_a, plane_a, line_a, gram_a)
            for q in range(NQ):
                m[rows_a * q : rows_a * (q + 1), :] = gram_a[it, q]

            @pl.when(it == 0)
            def _():
                for copy in edges():
                    copy.wait_recv()
                for copy in passes((me, 1)):
                    copy.start()

        @pl.when(core == 1)
        def _():
            y = y3[it, own, :]
            block = dot(y, y, ((0,), (0,)), HIGHEST)
            for q in range(NQ // 2):
                part_b[it, NQ // 2 + q] = block[rows_b * q : rows_b * (q + 1), :]
            take_y.wait_recv()
            block = dot(other[it, own, :], y, ((0,), (0,)), HIGHEST)
            for q in range(NQ // 2):
                part_b[it, q] = block[rows_b * q : rows_b * (q + 1), :]
            sum_over_rows(it, part_b, plane_b, line_b, gram_b)
            take_w.wait_recv()
            gab = gram_b[it, 0 : NQ // 2].reshape(TILE, TILE)
            gbb = gram_b[it, NQ // 2 :].reshape(TILE, TILE)
            cab = dot(waa[it], gab, ((1,), (0,)), HIGHEST)
            m[...] = gbb - dot(cab, cab, ((0,), (0,)), HIGHEST)
            shift[...] = dot(waa[it], cab, ((0,), (0,)), HIGHEST)

        for g, group in enumerate(inverse_factor([m[8 * i : 8 * i + 8, :] for i in range(16)])):
            w[it, 8 * g : 8 * g + 8, :] = group

        def update(new_rows, arrive):
            x[...] = new_rows(own)

            @pl.when(it == 0)
            def _():
                z[DEGREE, own, :] = x[...].astype(BF16)
                arrive()
                for rows in (slice(0, LOW), slice(LOW + OWN, EXT)):
                    z[DEGREE, rows, :] = new_rows(rows).astype(BF16)

        @pl.when(core == 0)
        def _():
            give_w.start()
            update(lambda rows: dot(y3[it, rows, :], w[it], ((1,), (1,)), HIGHEST), lambda: None)
            give_y.wait_send()
            give_w.wait_send()

            @pl.when(it == 0)
            def _():
                for copy in passes((me, 1)):
                    copy.wait_send()

        @pl.when(core == 1)
        def _():
            wba[...] = -dot(w[it], shift[...], ((1,), (1,)), HIGHEST)

            def new_rows(rows):
                both = jnp.concatenate([y3[it, rows, :], other[it, rows, :]], axis=1)
                return dot(both, jnp.concatenate([w[it], wba[...]], axis=1), ((1,), (1,)), HIGHEST)

            def arrive():
                for copy in [*edges(), *passes((me, 0))]:
                    copy.wait_recv()

            update(new_rows, arrive)

        @pl.when(it == 0)
        def _():
            for copy in [*halo(0), *edges()]:
                copy.wait_send()

        for step in range(1, DEGREE):
            for copy in halo(first + step):
                copy.wait_send()
        return carry

    lax.fori_loop(0, ITERS, iteration, 0)
    out_ref[...] = x[...]


def per_device(axes, start, tiles, tile_cols):
    NZ, NX, NY = axes
    NQ = NX * NY
    rows_a, rows_b = TILE // NQ, 2 * TILE // NQ
    dma = pltpu.SemaphoreType.DMA
    steps = ITERS * DEGREE

    def vmem(*shape, dtype=F32):
        return pltpu.VMEM(shape, dtype)

    return pl.pallas_call(
        functools.partial(kernel, axes),
        out_shape=jax.ShapeDtypeStruct((OWN, TILE), F32),
        in_specs=[pl.BlockSpec(memory_space=pltpu.SMEM), ANY, ANY],
        out_specs=pl.BlockSpec(memory_space=pltpu.VMEM),
        scratch_shapes=[
            vmem(BR * TPR, TILE, TILE, dtype=BF16),
            vmem(2, OWN, EXT, dtype=BF16),
            vmem(OWN, TILE),
            vmem(steps, EXT, TILE, dtype=BF16),
            vmem(OWN, TILE), vmem(OWN, TILE), vmem(ITERS, EXT, TILE), vmem(ITERS, EXT, TILE),
            vmem(TILE, TILE), vmem(ITERS, TILE, TILE), vmem(ITERS, TILE, TILE), vmem(TILE, TILE), vmem(TILE, TILE),
            vmem(ITERS, NQ, rows_a, TILE), vmem(ITERS, NQ, rows_b, TILE),
            vmem(ITERS, NQ, rows_a, TILE), vmem(ITERS, NQ, rows_b, TILE),
            vmem(ITERS, NZ, rows_a, TILE), vmem(ITERS, NZ, rows_b, TILE),
            vmem(ITERS, NQ, rows_a, TILE), vmem(ITERS, NQ, rows_b, TILE),
            dma((2,)), dma((steps, 2)), dma((steps, 2)), dma((ITERS, 2)), dma((ITERS, 2)),
            dma((2,)), dma((2,)), dma((2,)), dma((2,)),
        ] + [dma((ITERS,))] * 6,
        compiler_params=pltpu.CompilerParams(collective_id=0, has_side_effects=True),
        name="embed",
    )(tile_cols, start, tiles)


def solution(mesh, axes=AXES):
    placed = (P("rows", "cols"), P("rows", None, None), P("rows"))
    return jax.shard_map(
        functools.partial(per_device, axes),
        mesh=mesh, in_specs=placed, out_specs=P("rows", "cols"), check_vma=False,
    )
```

```python
import functools

import jax
import jax.numpy as jnp
from jax import lax
from jax.experimental import pallas as pl
from jax.experimental.pallas import tpu as pltpu
from jax.sharding import PartitionSpec as P

TILE = 128
BR = 3
TPR = 12
CUT = 2
SPAN = BR + 2 * CUT
DEGREE = 3
ITERS = 2
OWN = BR * TILE
EXT = SPAN * TILE
LOW = CUT * TILE
AXES = (12, 4, 8)
MESH = pl.DeviceIdType.MESH
ANY = pl.BlockSpec(memory_space=pl.ANY)
F32 = jnp.float32
BF16 = jnp.bfloat16
HIGHEST = lax.Precision.HIGHEST


def dot(a, b, contract, precision=None):
    return lax.dot_general(
        a, b, (contract, ((), ())), precision=precision, preferred_element_type=F32
    )


def lane_copy(v, c):
    return jnp.broadcast_to(v[:, c : c + 1], (8, TILE))


def row_copy(v, r):
    return jnp.broadcast_to(v[r : r + 1, :], (8, TILE))


def inverse_factor(m):
    lane = lax.broadcasted_iota(jnp.int32, (8, TILE), 1)
    sub = lax.broadcasted_iota(jnp.int32, (8, TILE), 0)
    m = list(m)
    w = [None] * 16
    for g in range(16):
        first = 8 * g
        spread = [lane_copy(m[g], first + k) for k in range(8)]
        a = [[row_copy(spread[k], i) if i >= k else None for k in range(8)] for i in range(8)]
        inside = (lane >= first) & (lane < first + 8)
        rows = jnp.where(inside, jnp.where(lane == sub + first, 1.0, 0.0), m[g])
        r = [None] * 8
        c = [[None] * 8 for _ in range(8)]
        for k in range(8):
            r[k] = lax.rsqrt(a[k][k])
            for i in range(k + 1, 8):
                c[i][k] = a[i][k] * r[k]
            for j in range(k + 1, 8):
                for i in range(j, 8):
                    a[i][j] = a[i][j] - c[i][k] * c[j][k]
        solved = [row_copy(rows, k) for k in range(8)]
        for k in range(8):
            solved[k] = solved[k] * r[k]
            for j in range(k + 1, 8):
                solved[j] = solved[j] - c[j][k] * solved[k]
        group = solved[0]
        for k in range(1, 8):
            group = jnp.where(sub == k, solved[k], group)
        w[g] = jnp.where(lane < first + 8, group, 0.0)
        for i in range(g + 1, 16):
            p = [lane_copy(m[i], first + k) for k in range(8)]
            rest = jnp.where(inside, 0.0, m[i])
            for k in range(8):
                col = p[k] * r[k]
                for j in range(k + 1, 8):
                    p[j] = p[j] - c[j][k] * col
                rest = rest - col * solved[k]
            m[i] = rest
    return w


def kernel(
    axes, cols_ref, x_ref, tiles_ref, last_y, last_w,
    tiles, band, x, z, y1, y2, y3, other, m, w, waa, shift, wba,
    part_a, part_b, plane_a, plane_b, line_a, line_b, gram_a, gram_b,
    load, store, halo_s, halo_r, pair_s, pair_r, edge_s, edge_r, pass_s, pass_r, plane_s, plane_r, line_s, line_r, gram_s, gram_r,
):
    NZ, NX, NY = axes
    NQ = NX * NY
    me = lax.axis_index("rows")
    core = lax.axis_index("cols")
    my_z, my_q = me // NQ, me % NQ
    my_x, my_y = my_q // NY, my_q % NY
    count = NZ * NQ
    right, left = lax.rem(me + 1, count), lax.rem(me + count - 1, count)
    has_left, has_right = me > 0, me < count - 1
    steps = [(dx, dy) for dx in range(NX) for dy in range(NY) if dx or dy]
    steps.sort(key=lambda s: -min(s[0], NX - s[0]) - min(s[1], NY - s[1]))
    in_plane = [lax.rem(my_x + dx, NX) * NY + lax.rem(my_y + dy, NY) for dx, dy in steps]
    in_line = [lax.rem(my_z + d, NZ) for d in sorted(range(1, NZ), key=lambda d: -min(d, NZ - d))]
    load_x = pltpu.make_async_copy(x_ref, x, load.at[0])
    load_tiles = pltpu.make_async_copy(tiles_ref, tiles, load.at[1])
    load_x.start()
    load_tiles.start()

    barrier = pltpu.get_barrier_semaphore()
    greet = [(zz * NQ + my_q, core) for zz in in_line]
    greet += [(my_z * NQ + q, core) for q in in_plane]
    greet += [(left, core), (right, core), (me, 1 - core)]
    for device in greet:
        pl.semaphore_signal(barrier, inc=1, device_id=device, device_id_type=MESH)

    @pl.when(me == 0)
    def _():
        z[:, 0:LOW, :] = jnp.zeros((ITERS * DEGREE, LOW, TILE), BF16)
        y3[0, 0:LOW, :] = jnp.zeros((LOW, TILE), F32)

    @pl.when(me == count - 1)
    def _():
        z[:, LOW + OWN : EXT, :] = jnp.zeros((ITERS * DEGREE, LOW, TILE), BF16)
        y3[0, LOW + OWN : EXT, :] = jnp.zeros((LOW, TILE), F32)

    @pl.when(core == 0)
    def _():
        other[ITERS - 1, LOW : LOW + OWN, :] = jnp.zeros((OWN, TILE), F32)
        wba[...] = jnp.zeros((TILE, TILE), F32)

    load_x.wait()
    z[0, LOW : LOW + OWN, :] = x[...].astype(BF16)
    pl.semaphore_wait(barrier, len(greet))

    def remote(src, dst, send, recv, device):
        return pltpu.make_async_remote_copy(
            src_ref=src, dst_ref=dst, send_sem=send, recv_sem=recv,
            device_id=device, device_id_type=MESH,
        )

    def edges():
        down = remote(
            y3.at[0, pl.ds(LOW, LOW)], y3.at[0, pl.ds(LOW + OWN, LOW)], edge_s.at[0], edge_r.at[0], (left, core)
        )
        up = remote(y3.at[0, pl.ds(OWN, LOW)], y3.at[0, pl.ds(0, LOW)], edge_s.at[1], edge_r.at[1], (right, core))
        return down, up

    def passes(device):
        return [
            remote(y3.at[0, rows], other.at[0, rows], pass_s.at[i], pass_r.at[i], device)
            for i, rows in enumerate((pl.ds(0, LOW), pl.ds(LOW + OWN, LOW)))
        ]

    def halo(s):
        down = remote(
            z.at[s, pl.ds(LOW, LOW)], z.at[s, pl.ds(LOW + OWN, LOW)],
            halo_s.at[s, 0], halo_r.at[s, 0], (left, core),
        )
        up = remote(
            z.at[s, pl.ds(OWN, LOW)], z.at[s, pl.ds(0, LOW)],
            halo_s.at[s, 1], halo_r.at[s, 1], (right, core),
        )
        return down, up

    def begin(pair):
        pl.when(has_left)(pair[0].start)
        pl.when(has_right)(pair[1].start)

    def sent(pair):
        pl.when(has_left)(pair[0].wait_send)
        pl.when(has_right)(pair[1].wait_send)

    def arrived(pair):
        pl.when(has_right)(pair[0].wait_recv)
        pl.when(has_left)(pair[1].wait_recv)

    def band_dot(lanes, values):
        return dot(band[0, :, lanes], values, ((1,), (0,))) + dot(
            band[1, :, lanes], values, ((1,), (0,))
        )

    def apply(s, travelled=True):
        down, up = halo(s)
        product = band_dot(slice(LOW, LOW + OWN), z[s, LOW : LOW + OWN, :])
        pl.when(jnp.logical_and(travelled, has_left))(up.wait_recv)
        product += band_dot(slice(0, LOW), z[s, 0:LOW, :])
        pl.when(jnp.logical_and(travelled, has_right))(down.wait_recv)
        product += band_dot(slice(LOW + OWN, EXT), z[s, LOW + OWN : EXT, :])
        return product

    def send_on(s, value):
        z[s, LOW : LOW + OWN, :] = value.astype(BF16)
        begin(halo(s))

    begin(halo(0))
    load_tiles.wait()
    lowest = me * BR - CUT
    for r in range(BR):
        sums = [jnp.zeros((TILE, TILE), F32) for _ in range(SPAN)]
        for t in range(TPR):
            tile = tiles[r * TPR + t].astype(F32)
            place = cols_ref[r * TPR + t] - lowest
            for b in range(SPAN):
                sums[b] = sums[b] + jnp.where(place == b, tile, 0.0)
        for b in range(SPAN):
            high = sums[b].astype(BF16)
            rows = slice(r * TILE, (r + 1) * TILE)
            lanes = slice(b * TILE, (b + 1) * TILE)
            band[0, rows, lanes] = high
            band[1, rows, lanes] = (sums[b] - high.astype(F32)).astype(BF16)

    def sum_over_rows(it, part, plane, line, gram):
        for i, q in enumerate(in_plane):
            remote(
                part.at[it, q], plane.at[it, i + 1], plane_s.at[it], plane_r.at[it], (my_z * NQ + q, core)
            ).start()
        total = part[it, my_q]
        rest = pl.ds(1, NQ - 1)
        all_of_plane = remote(plane.at[it, rest], plane.at[it, rest], plane_s.at[it], plane_r.at[it], (me, 1 - core))
        all_of_plane.wait_recv()
        for i in range(1, NQ):
            total += plane[it, i]
        line[it, my_z] = total
        mine = line.at[it, my_z]
        for zz in in_line:
            remote(mine, mine, line_s.at[it], line_r.at[it], (zz * NQ + my_q, core)).start()

        @pl.when(it == 0)
        def _():
            begin(edges())

        rest = pl.ds(0, NZ - 1)
        all_of_line = remote(line.at[it, rest], line.at[it, rest], line_s.at[it], line_r.at[it], (me, 1 - core))
        all_of_line.wait_recv()
        total = line[it, 0]
        for i in range(1, NZ):
            total += line[it, i]
        gram[it, my_q] = total / (count * OWN)
        mine = gram.at[it, my_q]
        for q in in_plane:
            remote(mine, mine, gram_s.at[it], gram_r.at[it], (my_z * NQ + q, core)).start()
        rest = pl.ds(0, NQ - 1)
        all_of_gram = remote(gram.at[it, rest], gram.at[it, rest], gram_s.at[it], gram_r.at[it], (me, 1 - core))
        all_of_gram.wait_recv()
        for copy in (all_of_plane, all_of_line, all_of_gram):
            copy.wait_send()

    def iteration(it, carry):
        first = it * DEGREE

        own = slice(LOW, LOW + OWN)
        y1[...] = ((1.0 - 1.25) * x[...] - apply(first, it == 0)) / 0.75
        send_on(first + 1, y1[...])
        y2[...] = 2.0 * ((1.0 - 1.25) * y1[...] - apply(first + 1)) / 0.75 - x[...]
        send_on(first + 2, y2[...])
        y3[it, own, :] = 2.0 * ((1.0 - 1.25) * y2[...] - apply(first + 2)) / 0.75 - y1[...]
        give_y = remote(y3.at[it, pl.ds(LOW, OWN)], other.at[it, pl.ds(LOW, OWN)], pair_s.at[it, 0], pair_r.at[it, 0], (me, 1))
        give_w = remote(w.at[it], waa.at[it], pair_s.at[it, 1], pair_r.at[it, 1], (me, 1))
        take_y = remote(y3.at[it, pl.ds(LOW, OWN)], other.at[it, pl.ds(LOW, OWN)], pair_s.at[it, 0], pair_r.at[it, 0], (me, 0))
        take_w = remote(w.at[it], waa.at[it], pair_s.at[it, 1], pair_r.at[it, 1], (me, 0))
        rows_a, rows_b = TILE // NQ, 2 * TILE // NQ

        @pl.when(core == 0)
        def _():
            give_y.start()
            y = y3[it, own, :]
            block = dot(y, y, ((0,), (0,)), HIGHEST)
            for q in range(NQ):
                part_a[it, q] = block[rows_a * q : rows_a * (q + 1), :]
            sum_over_rows(it, part_a, plane_a, line_a, gram_a)
            for q in range(NQ):
                m[rows_a * q : rows_a * (q + 1), :] = gram_a[it, q]

            @pl.when(it == 0)
            def _():
                arrived(edges())
                for copy in passes((me, 1)):
                    copy.start()

        @pl.when(core == 1)
        def _():
            y = y3[it, own, :]
            block = dot(y, y, ((0,), (0,)), HIGHEST)
            for q in range(NQ // 2):
                part_b[it, NQ // 2 + q] = block[rows_b * q : rows_b * (q + 1), :]
            take_y.wait_recv()
            block = dot(other[it, own, :], y, ((0,), (0,)), HIGHEST)
            for q in range(NQ // 2):
                part_b[it, q] = block[rows_b * q : rows_b * (q + 1), :]
            sum_over_rows(it, part_b, plane_b, line_b, gram_b)
            take_w.wait_recv()
            gab = gram_b[it, 0 : NQ // 2].reshape(TILE, TILE)
            gbb = gram_b[it, NQ // 2 :].reshape(TILE, TILE)
            cab = dot(waa[it], gab, ((1,), (0,)), HIGHEST)
            m[...] = gbb - dot(cab, cab, ((0,), (0,)), HIGHEST)
            shift[...] = dot(waa[it], cab, ((0,), (0,)), HIGHEST)

        own_rows = pl.ds(LOW, OWN)
        first_half, second_half = pl.ds(0, TILE), pl.ds(TILE, TILE)
        stores = [
            pltpu.make_async_copy(y3.at[ITERS - 1, own_rows], last_y.at[:, first_half], store.at[0]),
            pltpu.make_async_copy(other.at[ITERS - 1, own_rows], last_y.at[:, second_half], store.at[1]),
            pltpu.make_async_copy(w.at[ITERS - 1], last_w.at[:, first_half], store.at[2]),
            pltpu.make_async_copy(wba, last_w.at[:, second_half], store.at[3]),
        ]

        @pl.when(it == ITERS - 1)
        def _():
            stores[0].start()
            stores[1].start()

        for g, group in enumerate(inverse_factor([m[8 * i : 8 * i + 8, :] for i in range(16)])):
            w[it, 8 * g : 8 * g + 8, :] = group

        pl.when(it == ITERS - 1)(stores[2].start)

        def update(new_rows, arrive):
            @pl.when(it == 0)
            def _():
                x[...] = new_rows(own)
                z[DEGREE, own, :] = x[...].astype(BF16)
                arrive()
                for rows in (slice(0, LOW), slice(LOW + OWN, EXT)):
                    z[DEGREE, rows, :] = new_rows(rows).astype(BF16)

        @pl.when(core == 0)
        def _():
            give_w.start()
            update(lambda rows: dot(y3[it, rows, :], w[it], ((1,), (1,)), HIGHEST), lambda: None)
            give_y.wait_send()
            give_w.wait_send()

            @pl.when(it == 0)
            def _():
                for copy in passes((me, 1)):
                    copy.wait_send()

        @pl.when(core == 1)
        def _():
            wba[...] = -dot(w[it], shift[...], ((1,), (1,)), HIGHEST)

            def new_rows(rows):
                both = jnp.concatenate([y3[it, rows, :], other[it, rows, :]], axis=1)
                return dot(both, jnp.concatenate([w[it], wba[...]], axis=1), ((1,), (1,)), HIGHEST)

            def arrive():
                arrived(edges())
                for copy in passes((me, 0)):
                    copy.wait_recv()

            update(new_rows, arrive)

        @pl.when(it == ITERS - 1)
        def _():
            stores[3].start()
            for copy in stores:
                copy.wait()

        @pl.when(it == 0)
        def _():
            sent(halo(0))
            sent(edges())

        for step in range(1, DEGREE):
            sent(halo(first + step))
        return carry

    lax.fori_loop(0, ITERS, iteration, 0)


def per_device(axes, start, tiles, tile_cols):
    NZ, NX, NY = axes
    NQ = NX * NY
    rows_a, rows_b = TILE // NQ, 2 * TILE // NQ
    dma = pltpu.SemaphoreType.DMA
    steps = ITERS * DEGREE

    def vmem(*shape, dtype=F32):
        return pltpu.VMEM(shape, dtype)

    last_y, last_w = pl.pallas_call(
        functools.partial(kernel, axes),
        out_shape=(jax.ShapeDtypeStruct((OWN, 2 * TILE), F32), jax.ShapeDtypeStruct((TILE, 2 * TILE), F32)),
        in_specs=[pl.BlockSpec(memory_space=pltpu.SMEM), ANY, ANY],
        out_specs=(ANY, ANY),
        scratch_shapes=[
            vmem(BR * TPR, TILE, TILE, dtype=BF16),
            vmem(2, OWN, EXT, dtype=BF16),
            vmem(OWN, TILE),
            vmem(steps, EXT, TILE, dtype=BF16),
            vmem(OWN, TILE), vmem(OWN, TILE), vmem(ITERS, EXT, TILE), vmem(ITERS, EXT, TILE),
            vmem(TILE, TILE), vmem(ITERS, TILE, TILE), vmem(ITERS, TILE, TILE), vmem(TILE, TILE), vmem(TILE, TILE),
            vmem(ITERS, NQ, rows_a, TILE), vmem(ITERS, NQ, rows_b, TILE),
            vmem(ITERS, NQ, rows_a, TILE), vmem(ITERS, NQ, rows_b, TILE),
            vmem(ITERS, NZ, rows_a, TILE), vmem(ITERS, NZ, rows_b, TILE),
            vmem(ITERS, NQ, rows_a, TILE), vmem(ITERS, NQ, rows_b, TILE),
            dma((2,)), dma((4,)), dma((steps, 2)), dma((steps, 2)), dma((ITERS, 2)), dma((ITERS, 2)),
            dma((2,)), dma((2,)), dma((2,)), dma((2,)),
        ] + [dma((ITERS,))] * 6,
        compiler_params=pltpu.CompilerParams(collective_id=0, has_side_effects=True),
        name="embed",
    )(tile_cols, start, tiles)
    return dot(last_y, last_w, ((1,), (1,)), HIGHEST)


def solution(mesh, axes=AXES):
    placed = (P("rows", "cols"), P("rows", None, None), P("rows"))
    return jax.shard_map(
        functools.partial(per_device, axes),
        mesh=mesh, in_specs=placed, out_specs=P("rows", "cols"), check_vma=False,
    )
```

```python
import functools

import jax
import jax.numpy as jnp
from jax import lax
from jax.experimental import pallas as pl
from jax.experimental.pallas import tpu as pltpu
from jax.sharding import PartitionSpec as P

TILE = 128
BR = 3
TPR = 12
CUT = 2
SPAN = BR + 2 * CUT
DEGREE = 3
ITERS = 2
OWN = BR * TILE
EXT = SPAN * TILE
LOW = CUT * TILE
AXES = (12, 4, 8)
MESH = pl.DeviceIdType.MESH
ANY = pl.BlockSpec(memory_space=pl.ANY)
F32 = jnp.float32
BF16 = jnp.bfloat16
HIGHEST = lax.Precision.HIGHEST


def dot(a, b, contract, precision=None):
    return lax.dot_general(
        a, b, (contract, ((), ())), precision=precision, preferred_element_type=F32
    )


def lane_copy(v, c):
    return jnp.broadcast_to(v[:, c : c + 1], (8, TILE))


def row_copy(v, r):
    return jnp.broadcast_to(v[r : r + 1, :], (8, TILE))


def inverse_factor(m):
    lane = lax.broadcasted_iota(jnp.int32, (8, TILE), 1)
    sub = lax.broadcasted_iota(jnp.int32, (8, TILE), 0)
    m = list(m)
    w = [None] * 16
    for g in range(16):
        first = 8 * g
        spread = [lane_copy(m[g], first + k) for k in range(8)]
        a = [[row_copy(spread[k], i) if i >= k else None for k in range(8)] for i in range(8)]
        inside = (lane >= first) & (lane < first + 8)
        rows = jnp.where(inside, jnp.where(lane == sub + first, 1.0, 0.0), m[g])
        r = [None] * 8
        c = [[None] * 8 for _ in range(8)]
        for k in range(8):
            r[k] = lax.rsqrt(a[k][k])
            for i in range(k + 1, 8):
                c[i][k] = a[i][k] * r[k]
            for j in range(k + 1, 8):
                for i in range(j, 8):
                    a[i][j] = a[i][j] - c[i][k] * c[j][k]
        solved = [row_copy(rows, k) for k in range(8)]
        for k in range(8):
            solved[k] = solved[k] * r[k]
            for j in range(k + 1, 8):
                solved[j] = solved[j] - c[j][k] * solved[k]
        group = solved[0]
        for k in range(1, 8):
            group = jnp.where(sub == k, solved[k], group)
        w[g] = jnp.where(lane < first + 8, group, 0.0)
        for i in range(g + 1, 16):
            p = [lane_copy(m[i], first + k) for k in range(8)]
            rest = jnp.where(inside, 0.0, m[i])
            for k in range(8):
                col = p[k] * r[k]
                for j in range(k + 1, 8):
                    p[j] = p[j] - c[j][k] * col
                rest = rest - col * solved[k]
            m[i] = rest
    return w


def clear(ref, rows):
    ref[ITERS - 1, rows, :] = jnp.zeros((LOW, TILE), F32)


def kernel(
    axes, cols_hbm, x_ref, tiles_ref, last_y, last_w,
    cols_ref, tiles, band, x, z, y1, y2, y3, other, m, w, waa, cab, rest,
    part_a, part_b, plane_a, plane_b, line_a, line_b, gram_a, gram_b,
    load, store, halo_s, halo_r, pair_s, pair_r, edge_s, edge_r, pass_s, pass_r, plane_s, plane_r, line_s, line_r, gram_s, gram_r,
):
    NZ, NX, NY = axes
    NQ = NX * NY
    me = lax.axis_index("rows")
    core = lax.axis_index("cols")
    my_z, my_q = me // NQ, me % NQ
    my_x, my_y = my_q // NY, my_q % NY
    count = NZ * NQ
    right, left = lax.rem(me + 1, count), lax.rem(me + count - 1, count)
    has_left, has_right = me > 0, me < count - 1
    steps = [(dx, dy) for dx in range(NX) for dy in range(NY) if dx or dy]
    steps.sort(key=lambda s: -min(s[0], NX - s[0]) - min(s[1], NY - s[1]))
    in_plane = [lax.rem(my_x + dx, NX) * NY + lax.rem(my_y + dy, NY) for dx, dy in steps]
    in_line = [lax.rem(my_z + d, NZ) for d in sorted(range(1, NZ), key=lambda d: -min(d, NZ - d))]
    load_x = pltpu.make_async_copy(x_ref, x, load.at[0])
    load_tiles = pltpu.make_async_copy(tiles_ref, tiles, load.at[1])
    load_cols = pltpu.make_async_copy(cols_hbm, cols_ref, load.at[2])
    load_x.start()
    load_cols.start()
    load_tiles.start()

    barrier = pltpu.get_barrier_semaphore()
    greet = [(zz * NQ + my_q, core) for zz in in_line]
    greet += [(my_z * NQ + q, core) for q in in_plane]
    greet += [(left, core), (right, core), (me, 1 - core)]
    for device in greet:
        pl.semaphore_signal(barrier, inc=1, device_id=device, device_id_type=MESH)

    @pl.when(me == 0)
    def _():
        z[:, 0:LOW, :] = jnp.zeros((ITERS * DEGREE, LOW, TILE), BF16)
        y3[0, 0:LOW, :] = jnp.zeros((LOW, TILE), F32)

    @pl.when(me == count - 1)
    def _():
        z[:, LOW + OWN : EXT, :] = jnp.zeros((ITERS * DEGREE, LOW, TILE), BF16)
        y3[0, LOW + OWN : EXT, :] = jnp.zeros((LOW, TILE), F32)

    load_x.wait()
    z[0, LOW : LOW + OWN, :] = x[...].astype(BF16)
    pl.semaphore_wait(barrier, len(greet))

    def remote(src, dst, send, recv, device):
        return pltpu.make_async_remote_copy(
            src_ref=src, dst_ref=dst, send_sem=send, recv_sem=recv,
            device_id=device, device_id_type=MESH,
        )

    def edges():
        down = remote(
            y3.at[0, pl.ds(LOW, LOW)], y3.at[0, pl.ds(LOW + OWN, LOW)], edge_s.at[0], edge_r.at[0], (left, core)
        )
        up = remote(y3.at[0, pl.ds(OWN, LOW)], y3.at[0, pl.ds(0, LOW)], edge_s.at[1], edge_r.at[1], (right, core))
        return down, up

    def passes(device):
        return [
            remote(y3.at[0, rows], other.at[0, rows], pass_s.at[i], pass_r.at[i], device)
            for i, rows in enumerate((pl.ds(0, LOW), pl.ds(LOW + OWN, LOW)))
        ]

    def halo(s):
        down = remote(
            z.at[s, pl.ds(LOW, LOW)], z.at[s, pl.ds(LOW + OWN, LOW)],
            halo_s.at[s, 0], halo_r.at[s, 0], (left, core),
        )
        up = remote(
            z.at[s, pl.ds(OWN, LOW)], z.at[s, pl.ds(0, LOW)],
            halo_s.at[s, 1], halo_r.at[s, 1], (right, core),
        )
        return down, up

    def begin(pair):
        pl.when(has_left)(pair[0].start)
        pl.when(has_right)(pair[1].start)

    def sent(pair):
        pl.when(has_left)(pair[0].wait_send)
        pl.when(has_right)(pair[1].wait_send)

    def arrived(pair):
        pl.when(has_right)(pair[0].wait_recv)
        pl.when(has_left)(pair[1].wait_recv)

    def band_dot(lanes, values):
        return dot(band[0, :, lanes], values, ((1,), (0,))) + dot(
            band[1, :, lanes], values, ((1,), (0,))
        )

    def apply(s, travelled=True):
        down, up = halo(s)
        product = band_dot(slice(LOW, LOW + OWN), z[s, LOW : LOW + OWN, :])
        pl.when(jnp.logical_and(travelled, has_left))(up.wait_recv)
        product += band_dot(slice(0, LOW), z[s, 0:LOW, :])
        pl.when(jnp.logical_and(travelled, has_right))(down.wait_recv)
        product += band_dot(slice(LOW + OWN, EXT), z[s, LOW + OWN : EXT, :])
        return product

    def send_on(s, value):
        z[s, LOW : LOW + OWN, :] = value.astype(BF16)
        begin(halo(s))

    begin(halo(0))

    @pl.when(core == 0)
    def _():
        other[...] = jnp.zeros((ITERS, EXT, TILE), F32)
        waa[...] = jnp.zeros((ITERS, TILE, TILE), F32)
        cab[...] = jnp.zeros((TILE, TILE), F32)

    for rows in (slice(0, LOW), slice(LOW + OWN, EXT)):
        y3[ITERS - 1, rows, :] = jnp.zeros((LOW, TILE), F32)
        pl.when(core == 1)(functools.partial(clear, other, rows))
    load_cols.wait()
    load_tiles.wait()
    lowest = me * BR - CUT
    for r in range(BR):
        sums = [jnp.zeros((TILE, TILE), F32) for _ in range(SPAN)]
        for t in range(TPR):
            tile = tiles[r * TPR + t].astype(F32)
            place = cols_ref[r * TPR + t] - lowest
            for b in range(SPAN):
                sums[b] = sums[b] + jnp.where(place == b, tile, 0.0)
        for b in range(SPAN):
            high = sums[b].astype(BF16)
            rows = slice(r * TILE, (r + 1) * TILE)
            lanes = slice(b * TILE, (b + 1) * TILE)
            band[0, rows, lanes] = high
            band[1, rows, lanes] = (sums[b] - high.astype(F32)).astype(BF16)

    def sum_over_rows(it, part, plane, line, gram):
        for i, q in enumerate(in_plane):
            remote(
                part.at[it, q], plane.at[it, i + 1], plane_s.at[it], plane_r.at[it], (my_z * NQ + q, core)
            ).start()
        total = part[it, my_q]
        rest = pl.ds(1, NQ - 1)
        all_of_plane = remote(plane.at[it, rest], plane.at[it, rest], plane_s.at[it], plane_r.at[it], (me, 1 - core))
        all_of_plane.wait_recv()
        for i in range(1, NQ):
            total += plane[it, i]
        line[it, my_z] = total
        mine = line.at[it, my_z]
        for zz in in_line:
            remote(mine, mine, line_s.at[it], line_r.at[it], (zz * NQ + my_q, core)).start()

        @pl.when(it == 0)
        def _():
            begin(edges())

        rest = pl.ds(0, NZ - 1)
        all_of_line = remote(line.at[it, rest], line.at[it, rest], line_s.at[it], line_r.at[it], (me, 1 - core))
        all_of_line.wait_recv()
        total = line[it, 0]
        for i in range(1, NZ):
            total += line[it, i]
        gram[it, my_q] = total / (count * OWN)
        mine = gram.at[it, my_q]
        for q in in_plane:
            remote(mine, mine, gram_s.at[it], gram_r.at[it], (my_z * NQ + q, core)).start()
        rest = pl.ds(0, NQ - 1)
        all_of_gram = remote(gram.at[it, rest], gram.at[it, rest], gram_s.at[it], gram_r.at[it], (me, 1 - core))
        all_of_gram.wait_recv()
        for copy in (all_of_plane, all_of_line, all_of_gram):
            copy.wait_send()

    def iteration(it, carry):
        first = it * DEGREE

        own = slice(LOW, LOW + OWN)
        y1[...] = ((1.0 - 1.25) * x[...] - apply(first, it == 0)) / 0.75
        send_on(first + 1, y1[...])
        y2[...] = 2.0 * ((1.0 - 1.25) * y1[...] - apply(first + 1)) / 0.75 - x[...]
        send_on(first + 2, y2[...])
        y3[it, own, :] = 2.0 * ((1.0 - 1.25) * y2[...] - apply(first + 2)) / 0.75 - y1[...]
        give_y = remote(y3.at[it, pl.ds(LOW, OWN)], other.at[it, pl.ds(LOW, OWN)], pair_s.at[it, 0], pair_r.at[it, 0], (me, 1))
        give_w = remote(w.at[it], waa.at[it], pair_s.at[it, 1], pair_r.at[it, 1], (me, 1))
        take_y = remote(y3.at[it, pl.ds(LOW, OWN)], other.at[it, pl.ds(LOW, OWN)], pair_s.at[it, 0], pair_r.at[it, 0], (me, 0))
        take_w = remote(w.at[it], waa.at[it], pair_s.at[it, 1], pair_r.at[it, 1], (me, 0))
        rows_a, rows_b = TILE // NQ, 2 * TILE // NQ

        @pl.when(core == 0)
        def _():
            give_y.start()
            y = y3[it, own, :]
            block = dot(y, y, ((0,), (0,)), HIGHEST)
            for q in range(NQ):
                part_a[it, q] = block[rows_a * q : rows_a * (q + 1), :]
            sum_over_rows(it, part_a, plane_a, line_a, gram_a)
            for q in range(NQ):
                m[rows_a * q : rows_a * (q + 1), :] = gram_a[it, q]

            @pl.when(it == 0)
            def _():
                arrived(edges())
                for copy in passes((me, 1)):
                    copy.start()

        @pl.when(core == 1)
        def _():
            y = y3[it, own, :]
            block = dot(y, y, ((0,), (0,)), HIGHEST)
            for q in range(NQ // 2):
                part_b[it, NQ // 2 + q] = block[rows_b * q : rows_b * (q + 1), :]
            take_y.wait_recv()
            block = dot(other[it, own, :], y, ((0,), (0,)), HIGHEST)
            for q in range(NQ // 2):
                part_b[it, q] = block[rows_b * q : rows_b * (q + 1), :]
            sum_over_rows(it, part_b, plane_b, line_b, gram_b)
            take_w.wait_recv()
            gab = gram_b[it, 0 : NQ // 2].reshape(TILE, TILE)
            gbb = gram_b[it, NQ // 2 :].reshape(TILE, TILE)
            cab[...] = dot(waa[it], gab, ((1,), (0,)), HIGHEST)
            m[...] = gbb - dot(cab[...], cab[...], ((0,), (0,)), HIGHEST)

            @pl.when(it == 0)
            def _():
                arrived(edges())
                for copy in passes((me, 0)):
                    copy.wait_recv()

        shift = dot(waa[it], cab[...], ((0,), (0,)), HIGHEST)
        rest[...] = y3[it] - dot(other[it], shift, ((1,), (0,)), HIGHEST)
        for g, group in enumerate(inverse_factor([m[8 * i : 8 * i + 8, :] for i in range(16)])):
            w[it, 8 * g : 8 * g + 8, :] = group

        pl.when(core == 0)(give_w.start)

        @pl.when(it == ITERS - 1)
        def _():
            stores = [
                pltpu.make_async_copy(rest.at[pl.ds(LOW, OWN)], last_y, store.at[0]),
                pltpu.make_async_copy(w.at[ITERS - 1], last_w, store.at[1]),
            ]
            for copy in stores:
                copy.start()
            for copy in stores:
                copy.wait()

        @pl.when(it == 0)
        def _():
            new = dot(rest[...], w[it], ((1,), (1,)), HIGHEST)
            x[...] = new[own, :]
            z[DEGREE] = new.astype(BF16)

        @pl.when(core == 0)
        def _():
            give_y.wait_send()
            give_w.wait_send()

            @pl.when(it == 0)
            def _():
                for copy in passes((me, 1)):
                    copy.wait_send()

        @pl.when(it == 0)
        def _():
            sent(halo(0))
            sent(edges())

        for step in range(1, DEGREE):
            sent(halo(first + step))
        return carry

    lax.fori_loop(0, ITERS, iteration, 0)


def per_device(axes, start, tiles, tile_cols):
    NZ, NX, NY = axes
    NQ = NX * NY
    rows_a, rows_b = TILE // NQ, 2 * TILE // NQ
    dma = pltpu.SemaphoreType.DMA
    steps = ITERS * DEGREE

    def vmem(*shape, dtype=F32):
        return pltpu.VMEM(shape, dtype)

    last_y, last_w = pl.pallas_call(
        functools.partial(kernel, axes),
        out_shape=(jax.ShapeDtypeStruct((OWN, TILE), F32), jax.ShapeDtypeStruct((TILE, TILE), F32)),
        in_specs=[ANY, ANY, ANY],
        out_specs=(ANY, ANY),
        scratch_shapes=[
            pltpu.SMEM((BR * TPR,), jnp.int32),
            vmem(BR * TPR, TILE, TILE, dtype=BF16),
            vmem(2, OWN, EXT, dtype=BF16),
            vmem(OWN, TILE),
            vmem(steps, EXT, TILE, dtype=BF16),
            vmem(OWN, TILE), vmem(OWN, TILE), vmem(ITERS, EXT, TILE), vmem(ITERS, EXT, TILE),
            vmem(TILE, TILE), vmem(ITERS, TILE, TILE), vmem(ITERS, TILE, TILE), vmem(TILE, TILE), vmem(EXT, TILE),
            vmem(ITERS, NQ, rows_a, TILE), vmem(ITERS, NQ, rows_b, TILE),
            vmem(ITERS, NQ, rows_a, TILE), vmem(ITERS, NQ, rows_b, TILE),
            vmem(ITERS, NZ, rows_a, TILE), vmem(ITERS, NZ, rows_b, TILE),
            vmem(ITERS, NQ, rows_a, TILE), vmem(ITERS, NQ, rows_b, TILE),
            dma((3,)), dma((2,)), dma((steps, 2)), dma((steps, 2)), dma((ITERS, 2)), dma((ITERS, 2)),
            dma((2,)), dma((2,)), dma((2,)), dma((2,)),
        ] + [dma((ITERS,))] * 6,
        compiler_params=pltpu.CompilerParams(collective_id=0, has_side_effects=True),
        name="embed",
    )(tile_cols, start, tiles)
    return dot(last_y, last_w, ((1,), (1,)), HIGHEST)


def solution(mesh, axes=AXES):
    placed = (P("rows", "cols"), P("rows", None, None), P("rows"))
    return jax.shard_map(
        functools.partial(per_device, axes),
        mesh=mesh, in_specs=placed, out_specs=P("rows", "cols"), check_vma=False,
    )
```

```python
import functools

import jax
import jax.numpy as jnp
from jax import lax
from jax.experimental import pallas as pl
from jax.experimental.pallas import tpu as pltpu
from jax.sharding import PartitionSpec as P

TILE = 128
BR = 3
TPR = 12
CUT = 2
SPAN = BR + 2 * CUT
DEGREE = 3
ITERS = 2
OWN = BR * TILE
EXT = SPAN * TILE
LOW = CUT * TILE
AXES = (12, 4, 8)
MESH = pl.DeviceIdType.MESH
ANY = pl.BlockSpec(memory_space=pl.ANY)
F32 = jnp.float32
BF16 = jnp.bfloat16
HIGHEST = lax.Precision.HIGHEST


def dot(a, b, contract, precision=None):
    return lax.dot_general(
        a, b, (contract, ((), ())), precision=precision, preferred_element_type=F32
    )


def lane_copy(v, c):
    return jnp.broadcast_to(v[:, c : c + 1], (8, TILE))


def row_copy(v, r):
    return jnp.broadcast_to(v[r : r + 1, :], (8, TILE))


def inverse_factor(m):
    lane = lax.broadcasted_iota(jnp.int32, (8, TILE), 1)
    sub = lax.broadcasted_iota(jnp.int32, (8, TILE), 0)
    m = list(m)
    w = [None] * 16
    for g in range(16):
        first = 8 * g
        spread = [lane_copy(m[g], first + k) for k in range(8)]
        a = [[row_copy(spread[k], i) if i >= k else None for k in range(8)] for i in range(8)]
        inside = (lane >= first) & (lane < first + 8)
        rows = jnp.where(inside, jnp.where(lane == sub + first, 1.0, 0.0), m[g])
        r = [None] * 8
        c = [[None] * 8 for _ in range(8)]
        for k in range(8):
            r[k] = lax.rsqrt(a[k][k])
            for i in range(k + 1, 8):
                c[i][k] = a[i][k] * r[k]
            for j in range(k + 1, 8):
                for i in range(j, 8):
                    a[i][j] = a[i][j] - c[i][k] * c[j][k]
        solved = [row_copy(rows, k) for k in range(8)]
        for k in range(8):
            solved[k] = solved[k] * r[k]
            for j in range(k + 1, 8):
                solved[j] = solved[j] - c[j][k] * solved[k]
        group = solved[0]
        for k in range(1, 8):
            group = jnp.where(sub == k, solved[k], group)
        w[g] = jnp.where(lane < first + 8, group, 0.0)
        for i in range(g + 1, 16):
            p = [lane_copy(m[i], first + k) for k in range(8)]
            rest = jnp.where(inside, 0.0, m[i])
            for k in range(8):
                col = p[k] * r[k]
                for j in range(k + 1, 8):
                    p[j] = p[j] - c[j][k] * col
                rest = rest - col * solved[k]
            m[i] = rest
    return w


def clear(ref, rows):
    ref[ITERS - 1, rows, :] = jnp.zeros((LOW, TILE), F32)


def kernel(
    axes, cols_hbm, x_ref, tiles_ref, last_y, last_w,
    cols_ref, tiles, band, x, z, y1, y2, y3, other, m, w, waa, cab, rest,
    part_a, part_b, plane_a, plane_b, line_a, line_b, gram_a, gram_b,
    load, store, halo_s, halo_r, pair_s, pair_r, edge_s, edge_r, pass_s, pass_r, plane_s, plane_r, line_s, line_r, gram_s, gram_r,
):
    NZ, NX, NY = axes
    NQ = NX * NY
    me = lax.axis_index("rows")
    core = lax.axis_index("cols")
    my_z, my_q = me // NQ, me % NQ
    my_x, my_y = my_q // NY, my_q % NY
    count = NZ * NQ
    right, left = lax.rem(me + 1, count), lax.rem(me + count - 1, count)
    has_left, has_right = me > 0, me < count - 1
    steps = [(dx, dy) for dx in range(NX) for dy in range(NY) if dx or dy]
    steps.sort(key=lambda s: -min(s[0], NX - s[0]) - min(s[1], NY - s[1]))
    in_plane = [lax.rem(my_x + dx, NX) * NY + lax.rem(my_y + dy, NY) for dx, dy in steps]
    in_line = [lax.rem(my_z + d, NZ) for d in sorted(range(1, NZ), key=lambda d: -min(d, NZ - d))]
    load_x = pltpu.make_async_copy(x_ref, x, load.at[0])
    load_tiles = pltpu.make_async_copy(tiles_ref, tiles, load.at[1])
    load_cols = pltpu.make_async_copy(cols_hbm, cols_ref, load.at[2])
    load_x.start()
    load_cols.start()
    load_tiles.start()

    barrier = pltpu.get_barrier_semaphore()
    greet = [(zz * NQ + my_q, core) for zz in in_line]
    greet += [(my_z * NQ + q, core) for q in in_plane]
    greet += [(left, core), (right, core), (me, 1 - core)]
    for device in greet:
        pl.semaphore_signal(barrier, inc=1, device_id=device, device_id_type=MESH)

    @pl.when(me == 0)
    def _():
        z[:, 0:LOW, :] = jnp.zeros((ITERS * DEGREE, LOW, TILE), BF16)
        y3[0, 0:LOW, :] = jnp.zeros((LOW, TILE), F32)

    @pl.when(me == count - 1)
    def _():
        z[:, LOW + OWN : EXT, :] = jnp.zeros((ITERS * DEGREE, LOW, TILE), BF16)
        y3[0, LOW + OWN : EXT, :] = jnp.zeros((LOW, TILE), F32)

    load_x.wait()
    z[0, LOW : LOW + OWN, :] = x[...].astype(BF16)
    pl.semaphore_wait(barrier, len(greet))

    def remote(src, dst, send, recv, device):
        return pltpu.make_async_remote_copy(
            src_ref=src, dst_ref=dst, send_sem=send, recv_sem=recv,
            device_id=device, device_id_type=MESH,
        )

    def edges():
        down = remote(
            y3.at[0, pl.ds(LOW, LOW)], y3.at[0, pl.ds(LOW + OWN, LOW)], edge_s.at[0], edge_r.at[0], (left, core)
        )
        up = remote(y3.at[0, pl.ds(OWN, LOW)], y3.at[0, pl.ds(0, LOW)], edge_s.at[1], edge_r.at[1], (right, core))
        return down, up

    def passes(device):
        return [
            remote(y3.at[0, rows], other.at[0, rows], pass_s.at[i], pass_r.at[i], device)
            for i, rows in enumerate((pl.ds(0, LOW), pl.ds(LOW + OWN, LOW)))
        ]

    def halo(s):
        down = remote(
            z.at[s, pl.ds(LOW, LOW)], z.at[s, pl.ds(LOW + OWN, LOW)],
            halo_s.at[s, 0], halo_r.at[s, 0], (left, core),
        )
        up = remote(
            z.at[s, pl.ds(OWN, LOW)], z.at[s, pl.ds(0, LOW)],
            halo_s.at[s, 1], halo_r.at[s, 1], (right, core),
        )
        return down, up

    def begin(pair):
        pl.when(has_left)(pair[0].start)
        pl.when(has_right)(pair[1].start)

    def sent(pair):
        pl.when(has_left)(pair[0].wait_send)
        pl.when(has_right)(pair[1].wait_send)

    def arrived(pair):
        pl.when(has_right)(pair[0].wait_recv)
        pl.when(has_left)(pair[1].wait_recv)

    def band_dot(lanes, values):
        return dot(band[0, :, lanes], values, ((1,), (0,))) + dot(
            band[1, :, lanes], values, ((1,), (0,))
        )

    def apply(s, travelled=True):
        down, up = halo(s)
        product = band_dot(slice(LOW, LOW + OWN), z[s, LOW : LOW + OWN, :])
        pl.when(jnp.logical_and(travelled, has_left))(up.wait_recv)
        product += band_dot(slice(0, LOW), z[s, 0:LOW, :])
        pl.when(jnp.logical_and(travelled, has_right))(down.wait_recv)
        product += band_dot(slice(LOW + OWN, EXT), z[s, LOW + OWN : EXT, :])
        return product

    def send_on(s, value):
        z[s, LOW : LOW + OWN, :] = value.astype(BF16)
        begin(halo(s))

    begin(halo(0))

    @pl.when(core == 0)
    def _():
        other[...] = jnp.zeros((ITERS, EXT, TILE), F32)
        waa[...] = jnp.zeros((ITERS, TILE, TILE), F32)
        cab[...] = jnp.zeros((TILE, TILE), F32)

    for rows in (slice(0, LOW), slice(LOW + OWN, EXT)):
        y3[ITERS - 1, rows, :] = jnp.zeros((LOW, TILE), F32)
        pl.when(core == 1)(functools.partial(clear, other, rows))
    load_cols.wait()
    load_tiles.wait()
    lowest = me * BR - CUT
    for r in range(BR):
        sums = [jnp.zeros((TILE, TILE), F32) for _ in range(SPAN)]
        for t in range(TPR):
            tile = tiles[r * TPR + t].astype(F32)
            place = cols_ref[r * TPR + t] - lowest
            for b in range(SPAN):
                sums[b] = sums[b] + jnp.where(place == b, tile, 0.0)
        for b in range(SPAN):
            high = sums[b].astype(BF16)
            rows = slice(r * TILE, (r + 1) * TILE)
            lanes = slice(b * TILE, (b + 1) * TILE)
            band[0, rows, lanes] = high
            band[1, rows, lanes] = (sums[b] - high.astype(F32)).astype(BF16)

    def sum_over_rows(it, part, plane, line, gram):
        for i, q in enumerate(in_plane):
            remote(
                part.at[it, q], plane.at[it, i + 1], plane_s.at[it], plane_r.at[it], (my_z * NQ + q, core)
            ).start()
        total = part[it, my_q]
        rest = pl.ds(1, NQ - 1)
        all_of_plane = remote(plane.at[it, rest], plane.at[it, rest], plane_s.at[it], plane_r.at[it], (me, 1 - core))
        all_of_plane.wait_recv()
        for i in range(1, NQ):
            total += plane[it, i]
        line[it, my_z] = total
        mine = line.at[it, my_z]
        for zz in in_line:
            remote(mine, mine, line_s.at[it], line_r.at[it], (zz * NQ + my_q, core)).start()

        @pl.when(it == 0)
        def _():
            begin(edges())

        rest = pl.ds(0, NZ - 1)
        all_of_line = remote(line.at[it, rest], line.at[it, rest], line_s.at[it], line_r.at[it], (me, 1 - core))
        all_of_line.wait_recv()
        total = line[it, 0]
        for i in range(1, NZ):
            total += line[it, i]
        gram[it, my_q] = total / (count * OWN)
        mine = gram.at[it, my_q]
        for q in in_plane:
            remote(mine, mine, gram_s.at[it], gram_r.at[it], (my_z * NQ + q, core)).start()
        rest = pl.ds(0, NQ - 1)
        all_of_gram = remote(gram.at[it, rest], gram.at[it, rest], gram_s.at[it], gram_r.at[it], (me, 1 - core))
        all_of_gram.wait_recv()
        for copy in (all_of_plane, all_of_line, all_of_gram):
            copy.wait_send()

    def iteration(it, carry):
        first = it * DEGREE

        own = slice(LOW, LOW + OWN)
        y1[...] = ((1.0 - 1.25) * x[...] - apply(first, it == 0)) / 0.75
        send_on(first + 1, y1[...])
        y2[...] = 2.0 * ((1.0 - 1.25) * y1[...] - apply(first + 1)) / 0.75 - x[...]
        send_on(first + 2, y2[...])
        y3[it, own, :] = 2.0 * ((1.0 - 1.25) * y2[...] - apply(first + 2)) / 0.75 - y1[...]
        give_y = remote(y3.at[it, pl.ds(LOW, OWN)], other.at[it, pl.ds(LOW, OWN)], pair_s.at[it, 0], pair_r.at[it, 0], (me, 1))
        give_w = remote(w.at[it], waa.at[it], pair_s.at[it, 1], pair_r.at[it, 1], (me, 1))
        take_y = remote(y3.at[it, pl.ds(LOW, OWN)], other.at[it, pl.ds(LOW, OWN)], pair_s.at[it, 0], pair_r.at[it, 0], (me, 0))
        take_w = remote(w.at[it], waa.at[it], pair_s.at[it, 1], pair_r.at[it, 1], (me, 0))
        rows_a, rows_b = TILE // NQ, 2 * TILE // NQ

        @pl.when(core == 0)
        def _():
            give_y.start()
            y = y3[it, own, :]
            block = dot(y, y, ((0,), (0,)), HIGHEST)
            for q in range(NQ):
                part_a[it, q] = block[rows_a * q : rows_a * (q + 1), :]
            sum_over_rows(it, part_a, plane_a, line_a, gram_a)
            for q in range(NQ):
                m[rows_a * q : rows_a * (q + 1), :] = gram_a[it, q]

            @pl.when(it == 0)
            def _():
                arrived(edges())
                for copy in passes((me, 1)):
                    copy.start()

        @pl.when(core == 1)
        def _():
            y = y3[it, own, :]
            block = dot(y, y, ((0,), (0,)), HIGHEST)
            for q in range(NQ // 2):
                part_b[it, NQ // 2 + q] = block[rows_b * q : rows_b * (q + 1), :]
            take_y.wait_recv()
            block = dot(other[it, own, :], y, ((0,), (0,)), HIGHEST)
            for q in range(NQ // 2):
                part_b[it, q] = block[rows_b * q : rows_b * (q + 1), :]
            sum_over_rows(it, part_b, plane_b, line_b, gram_b)
            take_w.wait_recv()
            gab = gram_b[it, 0 : NQ // 2].reshape(TILE, TILE)
            gbb = gram_b[it, NQ // 2 :].reshape(TILE, TILE)
            cab[...] = dot(waa[it], gab, ((1,), (0,)), HIGHEST)
            m[...] = gbb - dot(cab[...], cab[...], ((0,), (0,)), HIGHEST)

            @pl.when(it == 0)
            def _():
                arrived(edges())
                for copy in passes((me, 0)):
                    copy.wait_recv()

        shift = dot(waa[it], cab[...], ((0,), (0,)), HIGHEST)
        rest[...] = y3[it] - dot(other[it], shift, ((1,), (0,)), HIGHEST)
        for g, group in enumerate(inverse_factor([m[8 * i : 8 * i + 8, :] for i in range(16)])):
            w[it, 8 * g : 8 * g + 8, :] = group

        pl.when(core == 0)(give_w.start)

        @pl.when(it == ITERS - 1)
        def _():
            stores = [
                pltpu.make_async_copy(rest.at[pl.ds(LOW, OWN)], last_y, store.at[0]),
                pltpu.make_async_copy(w.at[ITERS - 1], last_w, store.at[1]),
            ]
            for copy in stores:
                copy.start()
            for copy in stores:
                copy.wait()

        @pl.when(it == 0)
        def _():
            new = dot(rest[...], w[it], ((1,), (1,)), HIGHEST)
            x[...] = new[own, :]
            z[DEGREE] = new.astype(BF16)

        @pl.when(core == 0)
        def _():
            give_y.wait_send()
            give_w.wait_send()

            @pl.when(it == 0)
            def _():
                for copy in passes((me, 1)):
                    copy.wait_send()

        @pl.when(it == 0)
        def _():
            sent(halo(0))
            sent(edges())

        for step in range(1, DEGREE):
            sent(halo(first + step))
        return carry

    lax.fori_loop(0, ITERS, iteration, 0)


def per_device(axes, start, tiles, tile_cols):
    NZ, NX, NY = axes
    NQ = NX * NY
    rows_a, rows_b = TILE // NQ, 2 * TILE // NQ
    dma = pltpu.SemaphoreType.DMA
    steps = ITERS * DEGREE

    def vmem(*shape, dtype=F32):
        return pltpu.VMEM(shape, dtype)

    last_y, last_w = pl.pallas_call(
        functools.partial(kernel, axes),
        out_shape=(jax.ShapeDtypeStruct((OWN, TILE), F32), jax.ShapeDtypeStruct((TILE, TILE), F32)),
        in_specs=[pl.BlockSpec(memory_space=pltpu.HBM)] * 3,
        out_specs=(ANY, ANY),
        scratch_shapes=[
            pltpu.SMEM((BR * TPR,), jnp.int32),
            vmem(BR * TPR, TILE, TILE, dtype=BF16),
            vmem(2, OWN, EXT, dtype=BF16),
            vmem(OWN, TILE),
            vmem(steps, EXT, TILE, dtype=BF16),
            vmem(OWN, TILE), vmem(OWN, TILE), vmem(ITERS, EXT, TILE), vmem(ITERS, EXT, TILE),
            vmem(TILE, TILE), vmem(ITERS, TILE, TILE), vmem(ITERS, TILE, TILE), vmem(TILE, TILE), vmem(EXT, TILE),
            vmem(ITERS, NQ, rows_a, TILE), vmem(ITERS, NQ, rows_b, TILE),
            vmem(ITERS, NQ, rows_a, TILE), vmem(ITERS, NQ, rows_b, TILE),
            vmem(ITERS, NZ, rows_a, TILE), vmem(ITERS, NZ, rows_b, TILE),
            vmem(ITERS, NQ, rows_a, TILE), vmem(ITERS, NQ, rows_b, TILE),
            dma((3,)), dma((2,)), dma((steps, 2)), dma((steps, 2)), dma((ITERS, 2)), dma((ITERS, 2)),
            dma((2,)), dma((2,)), dma((2,)), dma((2,)),
        ] + [dma((ITERS,))] * 6,
        compiler_params=pltpu.CompilerParams(
            collective_id=0, has_side_effects=True, vmem_limit_bytes=24 * 2**20
        ),
        name="embed",
    )(*[pltpu.with_memory_space_constraint(a, pltpu.HBM) for a in (tile_cols, start, tiles)])
    return dot(last_y, last_w, ((1,), (1,)), HIGHEST)


def solution(mesh, axes=AXES):
    placed = (P("rows", "cols"), P("rows", None, None), P("rows"))
    return jax.shard_map(
        functools.partial(per_device, axes),
        mesh=mesh, in_specs=placed, out_specs=P("rows", "cols"), check_vma=False,
    )
```

```python
import functools

import jax
import jax.numpy as jnp
from jax import lax
from jax.experimental import pallas as pl
from jax.experimental.pallas import tpu as pltpu
from jax.sharding import PartitionSpec as P

TILE = 128
BR = 3
TPR = 12
CUT = 2
SPAN = BR + 2 * CUT
DEGREE = 3
ITERS = 2
OWN = BR * TILE
EXT = SPAN * TILE
LOW = CUT * TILE
AXES = (12, 4, 8)
MESH = pl.DeviceIdType.MESH
ANY = pl.BlockSpec(memory_space=pl.ANY)
F32 = jnp.float32
BF16 = jnp.bfloat16
HIGHEST = lax.Precision.HIGHEST


def dot(a, b, contract, precision=None):
    return lax.dot_general(
        a, b, (contract, ((), ())), precision=precision, preferred_element_type=F32
    )


def lane_copy(v, c):
    return jnp.broadcast_to(v[:, c : c + 1], (8, TILE))


def row_copy(v, r):
    return jnp.broadcast_to(v[r : r + 1, :], (8, TILE))


def inverse_factor(m):
    lane = lax.broadcasted_iota(jnp.int32, (8, TILE), 1)
    sub = lax.broadcasted_iota(jnp.int32, (8, TILE), 0)
    m = list(m)
    w = [None] * 16
    for g in range(16):
        first = 8 * g
        spread = [lane_copy(m[g], first + k) for k in range(8)]
        a = [[row_copy(spread[k], i) if i >= k else None for k in range(8)] for i in range(8)]
        inside = (lane >= first) & (lane < first + 8)
        rows = jnp.where(inside, jnp.where(lane == sub + first, 1.0, 0.0), m[g])
        r = [None] * 8
        c = [[None] * 8 for _ in range(8)]
        for k in range(8):
            r[k] = lax.rsqrt(a[k][k])
            for i in range(k + 1, 8):
                c[i][k] = a[i][k] * r[k]
            for j in range(k + 1, 8):
                for i in range(j, 8):
                    a[i][j] = a[i][j] - c[i][k] * c[j][k]
        solved = [row_copy(rows, k) for k in range(8)]
        for k in range(8):
            solved[k] = solved[k] * r[k]
            for j in range(k + 1, 8):
                solved[j] = solved[j] - c[j][k] * solved[k]
        group = solved[0]
        for k in range(1, 8):
            group = jnp.where(sub == k, solved[k], group)
        w[g] = jnp.where(lane < first + 8, group, 0.0)
        for i in range(g + 1, 16):
            p = [lane_copy(m[i], first + k) for k in range(8)]
            rest = jnp.where(inside, 0.0, m[i])
            for k in range(8):
                col = p[k] * r[k]
                for j in range(k + 1, 8):
                    p[j] = p[j] - c[j][k] * col
                rest = rest - col * solved[k]
            m[i] = rest
    return w


def clear(ref, rows):
    ref[ITERS - 1, rows, :] = jnp.zeros((LOW, TILE), F32)


def kernel(
    axes, cols_hbm, x_ref, tiles_ref, last_y, last_w,
    cols_ref, tiles, band, x, z, y1, y2, y3, other, m, w, waa, cab, rest,
    part_a, part_b, plane_a, plane_b, line_a, line_b, gram_a, gram_b,
    load, store, halo_s, halo_r, pair_s, pair_r, edge_s, edge_r, pass_s, pass_r, plane_s, plane_r, line_s, line_r, gram_s, gram_r,
):
    NZ, NX, NY = axes
    NQ = NX * NY
    me = lax.axis_index("rows")
    core = lax.axis_index("cols")
    my_z, my_q = me // NQ, me % NQ
    my_x, my_y = my_q // NY, my_q % NY
    count = NZ * NQ
    right, left = lax.rem(me + 1, count), lax.rem(me + count - 1, count)
    has_left, has_right = me > 0, me < count - 1
    steps = [(dx, dy) for dx in range(NX) for dy in range(NY) if dx or dy]
    steps.sort(key=lambda s: -min(s[0], NX - s[0]) - min(s[1], NY - s[1]))
    in_plane = [lax.rem(my_x + dx, NX) * NY + lax.rem(my_y + dy, NY) for dx, dy in steps]
    in_line = [lax.rem(my_z + d, NZ) for d in sorted(range(1, NZ), key=lambda d: -min(d, NZ - d))]
    load_x = pltpu.make_async_copy(x_ref, x, load.at[0])
    load_tiles = pltpu.make_async_copy(tiles_ref, tiles, load.at[1])
    load_cols = pltpu.make_async_copy(cols_hbm, cols_ref, load.at[2])
    load_x.start()
    load_cols.start()
    load_tiles.start()

    barrier = pltpu.get_barrier_semaphore()
    greet = [(zz * NQ + my_q, core) for zz in in_line]
    greet += [(my_z * NQ + q, core) for q in in_plane]
    greet += [(left, core), (right, core), (me, 1 - core)]
    for device in greet:
        pl.semaphore_signal(barrier, inc=1, device_id=device, device_id_type=MESH)

    @pl.when(me == 0)
    def _():
        z[:, 0:LOW, :] = jnp.zeros((ITERS * DEGREE, LOW, TILE), BF16)
        y3[0, 0:LOW, :] = jnp.zeros((LOW, TILE), F32)

    @pl.when(me == count - 1)
    def _():
        z[:, LOW + OWN : EXT, :] = jnp.zeros((ITERS * DEGREE, LOW, TILE), BF16)
        y3[0, LOW + OWN : EXT, :] = jnp.zeros((LOW, TILE), F32)

    load_x.wait()
    z[0, LOW : LOW + OWN, :] = x[...].astype(BF16)
    pl.semaphore_wait(barrier, len(greet))

    def remote(src, dst, send, recv, device):
        return pltpu.make_async_remote_copy(
            src_ref=src, dst_ref=dst, send_sem=send, recv_sem=recv,
            device_id=device, device_id_type=MESH,
        )

    def edges():
        down = remote(
            y3.at[0, pl.ds(LOW, LOW)], y3.at[0, pl.ds(LOW + OWN, LOW)], edge_s.at[0], edge_r.at[0], (left, core)
        )
        up = remote(y3.at[0, pl.ds(OWN, LOW)], y3.at[0, pl.ds(0, LOW)], edge_s.at[1], edge_r.at[1], (right, core))
        return down, up

    def passes(device):
        return [
            remote(y3.at[0, rows], other.at[0, rows], pass_s.at[i], pass_r.at[i], device)
            for i, rows in enumerate((pl.ds(0, LOW), pl.ds(LOW + OWN, LOW)))
        ]

    def halo(s):
        down = remote(
            z.at[s, pl.ds(LOW, LOW)], z.at[s, pl.ds(LOW + OWN, LOW)],
            halo_s.at[s, 0], halo_r.at[s, 0], (left, core),
        )
        up = remote(
            z.at[s, pl.ds(OWN, LOW)], z.at[s, pl.ds(0, LOW)],
            halo_s.at[s, 1], halo_r.at[s, 1], (right, core),
        )
        return down, up

    def begin(pair):
        pl.when(has_left)(pair[0].start)
        pl.when(has_right)(pair[1].start)

    def sent(pair):
        pl.when(has_left)(pair[0].wait_send)
        pl.when(has_right)(pair[1].wait_send)

    def arrived(pair):
        pl.when(has_right)(pair[0].wait_recv)
        pl.when(has_left)(pair[1].wait_recv)

    def band_dot(lanes, values):
        return dot(band[0, :, lanes], values, ((1,), (0,))) + dot(
            band[1, :, lanes], values, ((1,), (0,))
        )

    def apply(s, travelled=True):
        down, up = halo(s)
        product = band_dot(slice(LOW, LOW + OWN), z[s, LOW : LOW + OWN, :])
        pl.when(jnp.logical_and(travelled, has_left))(up.wait_recv)
        pl.when(jnp.logical_and(travelled, has_right))(down.wait_recv)
        product += band_dot(slice(0, LOW), z[s, 0:LOW, :])
        product += band_dot(slice(LOW + OWN, EXT), z[s, LOW + OWN : EXT, :])
        return product

    def send_on(s, value):
        z[s, LOW : LOW + OWN, :] = value.astype(BF16)
        begin(halo(s))

    begin(halo(0))

    @pl.when(core == 0)
    def _():
        other[...] = jnp.zeros((ITERS, EXT, TILE), F32)
        waa[...] = jnp.zeros((ITERS, TILE, TILE), F32)
        cab[...] = jnp.zeros((TILE, TILE), F32)

    for rows in (slice(0, LOW), slice(LOW + OWN, EXT)):
        y3[ITERS - 1, rows, :] = jnp.zeros((LOW, TILE), F32)
        pl.when(core == 1)(functools.partial(clear, other, rows))
    load_cols.wait()
    load_tiles.wait()
    lowest = me * BR - CUT
    for r in range(BR):
        sums = [jnp.zeros((TILE, TILE), F32) for _ in range(SPAN)]
        for t in range(TPR):
            tile = tiles[r * TPR + t].astype(F32)
            place = cols_ref[r * TPR + t] - lowest
            for b in range(SPAN):
                sums[b] = sums[b] + jnp.where(place == b, tile, 0.0)
        for b in range(SPAN):
            high = sums[b].astype(BF16)
            rows = slice(r * TILE, (r + 1) * TILE)
            lanes = slice(b * TILE, (b + 1) * TILE)
            band[0, rows, lanes] = high
            band[1, rows, lanes] = (sums[b] - high.astype(F32)).astype(BF16)

    def sum_over_rows(it, part, plane, line, gram):
        for i, q in enumerate(in_plane):
            remote(
                part.at[it, q], plane.at[it, i + 1], plane_s.at[it], plane_r.at[it], (my_z * NQ + q, core)
            ).start()
        total = part[it, my_q]
        rest = pl.ds(1, NQ - 1)
        all_of_plane = remote(plane.at[it, rest], plane.at[it, rest], plane_s.at[it], plane_r.at[it], (me, 1 - core))
        all_of_plane.wait_recv()
        for i in range(1, NQ):
            total += plane[it, i]
        line[it, my_z] = total
        mine = line.at[it, my_z]
        for zz in in_line:
            remote(mine, mine, line_s.at[it], line_r.at[it], (zz * NQ + my_q, core)).start()

        @pl.when(it == 0)
        def _():
            begin(edges())

        rest = pl.ds(0, NZ - 1)
        all_of_line = remote(line.at[it, rest], line.at[it, rest], line_s.at[it], line_r.at[it], (me, 1 - core))
        all_of_line.wait_recv()
        total = line[it, 0]
        for i in range(1, NZ):
            total += line[it, i]
        gram[it, my_q] = total / (count * OWN)
        mine = gram.at[it, my_q]
        for q in in_plane:
            remote(mine, mine, gram_s.at[it], gram_r.at[it], (my_z * NQ + q, core)).start()
        rest = pl.ds(0, NQ - 1)
        all_of_gram = remote(gram.at[it, rest], gram.at[it, rest], gram_s.at[it], gram_r.at[it], (me, 1 - core))
        all_of_gram.wait_recv()
        for copy in (all_of_plane, all_of_line, all_of_gram):
            copy.wait_send()

    def iteration(it, carry):
        first = it * DEGREE

        own = slice(LOW, LOW + OWN)
        y1[...] = ((1.0 - 1.25) * x[...] - apply(first, it == 0)) / 0.75
        send_on(first + 1, y1[...])
        y2[...] = 2.0 * ((1.0 - 1.25) * y1[...] - apply(first + 1)) / 0.75 - x[...]
        send_on(first + 2, y2[...])
        y3[it, own, :] = 2.0 * ((1.0 - 1.25) * y2[...] - apply(first + 2)) / 0.75 - y1[...]
        give_y = remote(y3.at[it, pl.ds(LOW, OWN)], other.at[it, pl.ds(LOW, OWN)], pair_s.at[it, 0], pair_r.at[it, 0], (me, 1))
        give_w = remote(w.at[it], waa.at[it], pair_s.at[it, 1], pair_r.at[it, 1], (me, 1))
        take_y = remote(y3.at[it, pl.ds(LOW, OWN)], other.at[it, pl.ds(LOW, OWN)], pair_s.at[it, 0], pair_r.at[it, 0], (me, 0))
        take_w = remote(w.at[it], waa.at[it], pair_s.at[it, 1], pair_r.at[it, 1], (me, 0))
        rows_a, rows_b = TILE // NQ, 2 * TILE // NQ

        @pl.when(core == 0)
        def _():
            give_y.start()
            y = y3[it, own, :]
            block = dot(y, y, ((0,), (0,)), HIGHEST)
            for q in range(NQ):
                part_a[it, q] = block[rows_a * q : rows_a * (q + 1), :]
            sum_over_rows(it, part_a, plane_a, line_a, gram_a)
            for q in range(NQ):
                m[rows_a * q : rows_a * (q + 1), :] = gram_a[it, q]

            @pl.when(it == 0)
            def _():
                arrived(edges())
                for copy in passes((me, 1)):
                    copy.start()

        @pl.when(core == 1)
        def _():
            y = y3[it, own, :]
            block = dot(y, y, ((0,), (0,)), HIGHEST)
            for q in range(NQ // 2):
                part_b[it, NQ // 2 + q] = block[rows_b * q : rows_b * (q + 1), :]
            take_y.wait_recv()
            block = dot(other[it, own, :], y, ((0,), (0,)), HIGHEST)
            for q in range(NQ // 2):
                part_b[it, q] = block[rows_b * q : rows_b * (q + 1), :]
            sum_over_rows(it, part_b, plane_b, line_b, gram_b)
            take_w.wait_recv()
            gab = gram_b[it, 0 : NQ // 2].reshape(TILE, TILE)
            gbb = gram_b[it, NQ // 2 :].reshape(TILE, TILE)
            cab[...] = dot(waa[it], gab, ((1,), (0,)), HIGHEST)
            m[...] = gbb - dot(cab[...], cab[...], ((0,), (0,)), HIGHEST)

            @pl.when(it == 0)
            def _():
                arrived(edges())
                for copy in passes((me, 0)):
                    copy.wait_recv()

        shift = dot(waa[it], cab[...], ((0,), (0,)), HIGHEST)
        rest[...] = y3[it] - dot(other[it], shift, ((1,), (0,)), HIGHEST)
        for g, group in enumerate(inverse_factor([m[8 * i : 8 * i + 8, :] for i in range(16)])):
            w[it, 8 * g : 8 * g + 8, :] = group

        pl.when(core == 0)(give_w.start)

        @pl.when(it == ITERS - 1)
        def _():
            stores = [
                pltpu.make_async_copy(rest.at[pl.ds(LOW, OWN)], last_y, store.at[0]),
                pltpu.make_async_copy(w.at[ITERS - 1], last_w, store.at[1]),
            ]
            for copy in stores:
                copy.start()
            for copy in stores:
                copy.wait()

        @pl.when(it == 0)
        def _():
            new = dot(rest[...], w[it], ((1,), (1,)), HIGHEST)
            x[...] = new[own, :]
            z[DEGREE] = new.astype(BF16)

        @pl.when(core == 0)
        def _():
            give_y.wait_send()
            give_w.wait_send()

            @pl.when(it == 0)
            def _():
                for copy in passes((me, 1)):
                    copy.wait_send()

        @pl.when(it == 0)
        def _():
            sent(halo(0))
            sent(edges())

        for step in range(1, DEGREE):
            sent(halo(first + step))
        return carry

    lax.fori_loop(0, ITERS, iteration, 0)


def per_device(axes, start, tiles, tile_cols):
    NZ, NX, NY = axes
    NQ = NX * NY
    rows_a, rows_b = TILE // NQ, 2 * TILE // NQ
    dma = pltpu.SemaphoreType.DMA
    steps = ITERS * DEGREE

    def vmem(*shape, dtype=F32):
        return pltpu.VMEM(shape, dtype)

    last_y, last_w = pl.pallas_call(
        functools.partial(kernel, axes),
        out_shape=(jax.ShapeDtypeStruct((OWN, TILE), F32), jax.ShapeDtypeStruct((TILE, TILE), F32)),
        in_specs=[pl.BlockSpec(memory_space=pltpu.HBM)] * 3,
        out_specs=(ANY, ANY),
        scratch_shapes=[
            pltpu.SMEM((BR * TPR,), jnp.int32),
            vmem(BR * TPR, TILE, TILE, dtype=BF16),
            vmem(2, OWN, EXT, dtype=BF16),
            vmem(OWN, TILE),
            vmem(steps, EXT, TILE, dtype=BF16),
            vmem(OWN, TILE), vmem(OWN, TILE), vmem(ITERS, EXT, TILE), vmem(ITERS, EXT, TILE),
            vmem(TILE, TILE), vmem(ITERS, TILE, TILE), vmem(ITERS, TILE, TILE), vmem(TILE, TILE), vmem(EXT, TILE),
            vmem(ITERS, NQ, rows_a, TILE), vmem(ITERS, NQ, rows_b, TILE),
            vmem(ITERS, NQ, rows_a, TILE), vmem(ITERS, NQ, rows_b, TILE),
            vmem(ITERS, NZ, rows_a, TILE), vmem(ITERS, NZ, rows_b, TILE),
            vmem(ITERS, NQ, rows_a, TILE), vmem(ITERS, NQ, rows_b, TILE),
            dma((3,)), dma((2,)), dma((steps, 2)), dma((steps, 2)), dma((ITERS, 2)), dma((ITERS, 2)),
            dma((2,)), dma((2,)), dma((2,)), dma((2,)),
        ] + [dma((ITERS,))] * 6,
        compiler_params=pltpu.CompilerParams(
            collective_id=0, has_side_effects=True, vmem_limit_bytes=24 * 2**20
        ),
        name="embed",
    )(*[pltpu.with_memory_space_constraint(a, pltpu.HBM) for a in (tile_cols, start, tiles)])
    return dot(last_y, last_w, ((1,), (1,)), HIGHEST)


def solution(mesh, axes=AXES):
    placed = (P("rows", "cols"), P("rows", None, None), P("rows"))
    return jax.shard_map(
        functools.partial(per_device, axes),
        mesh=mesh, in_specs=placed, out_specs=P("rows", "cols"), check_vma=False,
    )
```

```python
import functools

import jax
import jax.numpy as jnp
from jax import lax
from jax.experimental import pallas as pl
from jax.experimental.pallas import tpu as pltpu
from jax.sharding import PartitionSpec as P

TILE = 128
BR = 3
TPR = 12
CUT = 2
SPAN = BR + 2 * CUT
DEGREE = 3
ITERS = 2
OWN = BR * TILE
EXT = SPAN * TILE
LOW = CUT * TILE
AXES = (12, 4, 8)
MESH = pl.DeviceIdType.MESH
ANY = pl.BlockSpec(memory_space=pl.ANY)
F32 = jnp.float32
BF16 = jnp.bfloat16
HIGHEST = lax.Precision.HIGHEST


def dot(a, b, contract, precision=None):
    return lax.dot_general(
        a, b, (contract, ((), ())), precision=precision, preferred_element_type=F32
    )


def lane_copy(v, c):
    return jnp.broadcast_to(v[:, c : c + 1], (8, TILE))


def row_copy(v, r):
    return jnp.broadcast_to(v[r : r + 1, :], (8, TILE))


def inverse_factor(m):
    lane = lax.broadcasted_iota(jnp.int32, (8, TILE), 1)
    sub = lax.broadcasted_iota(jnp.int32, (8, TILE), 0)
    m = list(m)
    w = [None] * 16
    for g in range(16):
        first = 8 * g
        spread = [lane_copy(m[g], first + k) for k in range(8)]
        a = [[row_copy(spread[k], i) if i >= k else None for k in range(8)] for i in range(8)]
        inside = (lane >= first) & (lane < first + 8)
        rows = jnp.where(inside, jnp.where(lane == sub + first, 1.0, 0.0), m[g])
        r = [None] * 8
        c = [[None] * 8 for _ in range(8)]
        for k in range(8):
            r[k] = lax.rsqrt(a[k][k])
            for i in range(k + 1, 8):
                c[i][k] = a[i][k] * r[k]
            for j in range(k + 1, 8):
                for i in range(j, 8):
                    a[i][j] = a[i][j] - c[i][k] * c[j][k]
        solved = [row_copy(rows, k) for k in range(8)]
        for k in range(8):
            solved[k] = solved[k] * r[k]
            for j in range(k + 1, 8):
                solved[j] = solved[j] - c[j][k] * solved[k]
        group = solved[0]
        for k in range(1, 8):
            group = jnp.where(sub == k, solved[k], group)
        w[g] = jnp.where(lane < first + 8, group, 0.0)
        for i in range(g + 1, 16):
            p = [lane_copy(m[i], first + k) for k in range(8)]
            rest = jnp.where(inside, 0.0, m[i])
            for k in range(8):
                col = p[k] * r[k]
                for j in range(k + 1, 8):
                    p[j] = p[j] - c[j][k] * col
                rest = rest - col * solved[k]
            m[i] = rest
    return w


def clear(ref, rows):
    ref[ITERS - 1, rows, :] = jnp.zeros((LOW, TILE), F32)


def kernel(
    axes, cols_hbm, x_ref, tiles_ref, last_y, last_w,
    cols_ref, tiles, band, x, z, y1, y2, y3, other, m, w, waa, cab, rest,
    part_a, part_b, plane_a, plane_b, line_a, line_b, gram_a, gram_b,
    load, store, halo_s, halo_r, pair_s, pair_r, edge_s, edge_r, pass_s, pass_r, plane_s, plane_r, line_s, line_r, gram_s, gram_r,
):
    NZ, NX, NY = axes
    NQ = NX * NY
    me = lax.axis_index("rows")
    core = lax.axis_index("cols")
    my_z, my_q = me // NQ, me % NQ
    my_x, my_y = my_q // NY, my_q % NY
    count = NZ * NQ
    right, left = lax.rem(me + 1, count), lax.rem(me + count - 1, count)
    has_left, has_right = me > 0, me < count - 1
    steps = [(dx, dy) for dx in range(NX) for dy in range(NY) if dx or dy]
    steps.sort(key=lambda s: -min(s[0], NX - s[0]) - min(s[1], NY - s[1]))
    in_plane = [lax.rem(my_x + dx, NX) * NY + lax.rem(my_y + dy, NY) for dx, dy in steps]
    in_line = [lax.rem(my_z + d, NZ) for d in sorted(range(1, NZ), key=lambda d: -min(d, NZ - d))]
    load_x = pltpu.make_async_copy(x_ref, x, load.at[0])
    load_tiles = pltpu.make_async_copy(tiles_ref, tiles, load.at[1])
    load_cols = pltpu.make_async_copy(cols_hbm, cols_ref, load.at[2])
    load_x.start()
    load_cols.start()
    load_tiles.start()

    barrier = pltpu.get_barrier_semaphore()
    greet = [(zz * NQ + my_q, core) for zz in in_line]
    greet += [(my_z * NQ + q, core) for q in in_plane]
    greet += [(left, core), (right, core), (me, 1 - core)]
    for device in greet:
        pl.semaphore_signal(barrier, inc=1, device_id=device, device_id_type=MESH)

    @pl.when(me == 0)
    def _():
        z[:, 0:LOW, :] = jnp.zeros((ITERS * DEGREE, LOW, TILE), BF16)
        y3[0, 0:LOW, :] = jnp.zeros((LOW, TILE), F32)

    @pl.when(me == count - 1)
    def _():
        z[:, LOW + OWN : EXT, :] = jnp.zeros((ITERS * DEGREE, LOW, TILE), BF16)
        y3[0, LOW + OWN : EXT, :] = jnp.zeros((LOW, TILE), F32)

    load_x.wait()
    z[0, LOW : LOW + OWN, :] = x[...].astype(BF16)
    pl.semaphore_wait(barrier, len(greet))

    def remote(src, dst, send, recv, device):
        return pltpu.make_async_remote_copy(
            src_ref=src, dst_ref=dst, send_sem=send, recv_sem=recv,
            device_id=device, device_id_type=MESH,
        )

    def edges():
        down = remote(
            y3.at[0, pl.ds(LOW, LOW)], y3.at[0, pl.ds(LOW + OWN, LOW)], edge_s.at[0], edge_r.at[0], (left, core)
        )
        up = remote(y3.at[0, pl.ds(OWN, LOW)], y3.at[0, pl.ds(0, LOW)], edge_s.at[1], edge_r.at[1], (right, core))
        return down, up

    def passes(device):
        return [
            remote(y3.at[0, rows], other.at[0, rows], pass_s.at[i], pass_r.at[i], device)
            for i, rows in enumerate((pl.ds(0, LOW), pl.ds(LOW + OWN, LOW)))
        ]

    def halo(s):
        down = remote(
            z.at[s, pl.ds(LOW, LOW)], z.at[s, pl.ds(LOW + OWN, LOW)],
            halo_s.at[s, 0], halo_r.at[s, 0], (left, core),
        )
        up = remote(
            z.at[s, pl.ds(OWN, LOW)], z.at[s, pl.ds(0, LOW)],
            halo_s.at[s, 1], halo_r.at[s, 1], (right, core),
        )
        return down, up

    def begin(pair):
        pl.when(has_left)(pair[0].start)
        pl.when(has_right)(pair[1].start)

    def sent(pair):
        pl.when(has_left)(pair[0].wait_send)
        pl.when(has_right)(pair[1].wait_send)

    def arrived(pair):
        pl.when(has_right)(pair[0].wait_recv)
        pl.when(has_left)(pair[1].wait_recv)

    def band_dot(lanes, values):
        both = dot(band[:, :, lanes].reshape(2 * OWN, values.shape[0]), values, ((1,), (0,)))
        return both[:OWN] + both[OWN:]

    def apply(s, travelled=True):
        down, up = halo(s)
        product = band_dot(slice(LOW, LOW + OWN), z[s, LOW : LOW + OWN, :])
        pl.when(jnp.logical_and(travelled, has_left))(up.wait_recv)
        pl.when(jnp.logical_and(travelled, has_right))(down.wait_recv)
        product += band_dot(slice(0, LOW), z[s, 0:LOW, :])
        product += band_dot(slice(LOW + OWN, EXT), z[s, LOW + OWN : EXT, :])
        return product

    def send_on(s, value):
        z[s, LOW : LOW + OWN, :] = value.astype(BF16)
        begin(halo(s))

    begin(halo(0))

    @pl.when(core == 0)
    def _():
        other[...] = jnp.zeros((ITERS, EXT, TILE), F32)
        waa[...] = jnp.zeros((ITERS, TILE, TILE), F32)
        cab[...] = jnp.zeros((TILE, TILE), F32)

    for rows in (slice(0, LOW), slice(LOW + OWN, EXT)):
        y3[ITERS - 1, rows, :] = jnp.zeros((LOW, TILE), F32)
        pl.when(core == 1)(functools.partial(clear, other, rows))
    load_cols.wait()
    load_tiles.wait()
    lowest = me * BR - CUT
    for r in range(BR):
        sums = [jnp.zeros((TILE, TILE), F32) for _ in range(SPAN)]
        for t in range(TPR):
            tile = tiles[r * TPR + t].astype(F32)
            place = cols_ref[r * TPR + t] - lowest
            for b in range(SPAN):
                sums[b] = sums[b] + jnp.where(place == b, tile, 0.0)
        for b in range(SPAN):
            high = sums[b].astype(BF16)
            rows = slice(r * TILE, (r + 1) * TILE)
            lanes = slice(b * TILE, (b + 1) * TILE)
            band[0, rows, lanes] = high
            band[1, rows, lanes] = (sums[b] - high.astype(F32)).astype(BF16)

    def sum_over_rows(it, part, plane, line, gram):
        for i, q in enumerate(in_plane):
            remote(
                part.at[it, q], plane.at[it, i + 1], plane_s.at[it], plane_r.at[it], (my_z * NQ + q, core)
            ).start()
        total = part[it, my_q]
        rest = pl.ds(1, NQ - 1)
        all_of_plane = remote(plane.at[it, rest], plane.at[it, rest], plane_s.at[it], plane_r.at[it], (me, 1 - core))
        all_of_plane.wait_recv()
        for i in range(1, NQ):
            total += plane[it, i]
        line[it, my_z] = total
        mine = line.at[it, my_z]
        for zz in in_line:
            remote(mine, mine, line_s.at[it], line_r.at[it], (zz * NQ + my_q, core)).start()

        @pl.when(it == 0)
        def _():
            begin(edges())

        rest = pl.ds(0, NZ - 1)
        all_of_line = remote(line.at[it, rest], line.at[it, rest], line_s.at[it], line_r.at[it], (me, 1 - core))
        all_of_line.wait_recv()
        total = line[it, 0]
        for i in range(1, NZ):
            total += line[it, i]
        gram[it, my_q] = total / (count * OWN)
        mine = gram.at[it, my_q]
        for q in in_plane:
            remote(mine, mine, gram_s.at[it], gram_r.at[it], (my_z * NQ + q, core)).start()
        rest = pl.ds(0, NQ - 1)
        all_of_gram = remote(gram.at[it, rest], gram.at[it, rest], gram_s.at[it], gram_r.at[it], (me, 1 - core))
        all_of_gram.wait_recv()
        for copy in (all_of_plane, all_of_line, all_of_gram):
            copy.wait_send()

    def iteration(it, carry):
        first = it * DEGREE

        own = slice(LOW, LOW + OWN)
        y1[...] = ((1.0 - 1.25) * x[...] - apply(first, it == 0)) / 0.75
        send_on(first + 1, y1[...])
        y2[...] = 2.0 * ((1.0 - 1.25) * y1[...] - apply(first + 1)) / 0.75 - x[...]
        send_on(first + 2, y2[...])
        y3[it, own, :] = 2.0 * ((1.0 - 1.25) * y2[...] - apply(first + 2)) / 0.75 - y1[...]
        give_y = remote(y3.at[it, pl.ds(LOW, OWN)], other.at[it, pl.ds(LOW, OWN)], pair_s.at[it, 0], pair_r.at[it, 0], (me, 1))
        give_w = remote(w.at[it], waa.at[it], pair_s.at[it, 1], pair_r.at[it, 1], (me, 1))
        take_y = remote(y3.at[it, pl.ds(LOW, OWN)], other.at[it, pl.ds(LOW, OWN)], pair_s.at[it, 0], pair_r.at[it, 0], (me, 0))
        take_w = remote(w.at[it], waa.at[it], pair_s.at[it, 1], pair_r.at[it, 1], (me, 0))
        rows_a, rows_b = TILE // NQ, 2 * TILE // NQ

        @pl.when(core == 0)
        def _():
            give_y.start()
            y = y3[it, own, :]
            block = dot(y, y, ((0,), (0,)), HIGHEST)
            for q in range(NQ):
                part_a[it, q] = block[rows_a * q : rows_a * (q + 1), :]
            sum_over_rows(it, part_a, plane_a, line_a, gram_a)
            for q in range(NQ):
                m[rows_a * q : rows_a * (q + 1), :] = gram_a[it, q]

            @pl.when(it == 0)
            def _():
                arrived(edges())
                for copy in passes((me, 1)):
                    copy.start()

        @pl.when(core == 1)
        def _():
            y = y3[it, own, :]
            block = dot(y, y, ((0,), (0,)), HIGHEST)
            for q in range(NQ // 2):
                part_b[it, NQ // 2 + q] = block[rows_b * q : rows_b * (q + 1), :]
            take_y.wait_recv()
            block = dot(other[it, own, :], y, ((0,), (0,)), HIGHEST)
            for q in range(NQ // 2):
                part_b[it, q] = block[rows_b * q : rows_b * (q + 1), :]
            sum_over_rows(it, part_b, plane_b, line_b, gram_b)
            take_w.wait_recv()
            gab = gram_b[it, 0 : NQ // 2].reshape(TILE, TILE)
            gbb = gram_b[it, NQ // 2 :].reshape(TILE, TILE)
            cab[...] = dot(waa[it], gab, ((1,), (0,)), HIGHEST)
            m[...] = gbb - dot(cab[...], cab[...], ((0,), (0,)), HIGHEST)

            @pl.when(it == 0)
            def _():
                arrived(edges())
                for copy in passes((me, 0)):
                    copy.wait_recv()

        shift = dot(waa[it], cab[...], ((0,), (0,)), HIGHEST)
        rest[...] = y3[it] - dot(other[it], shift, ((1,), (0,)), HIGHEST)
        for g, group in enumerate(inverse_factor([m[8 * i : 8 * i + 8, :] for i in range(16)])):
            w[it, 8 * g : 8 * g + 8, :] = group

        pl.when(core == 0)(give_w.start)

        @pl.when(it == ITERS - 1)
        def _():
            stores = [
                pltpu.make_async_copy(rest.at[pl.ds(LOW, OWN)], last_y, store.at[0]),
                pltpu.make_async_copy(w.at[ITERS - 1], last_w, store.at[1]),
            ]
            for copy in stores:
                copy.start()
            for copy in stores:
                copy.wait()

        @pl.when(it == 0)
        def _():
            new = dot(rest[...], w[it], ((1,), (1,)), HIGHEST)
            x[...] = new[own, :]
            z[DEGREE] = new.astype(BF16)

        @pl.when(core == 0)
        def _():
            give_y.wait_send()
            give_w.wait_send()

            @pl.when(it == 0)
            def _():
                for copy in passes((me, 1)):
                    copy.wait_send()

        @pl.when(it == 0)
        def _():
            sent(halo(0))
            sent(edges())

        for step in range(1, DEGREE):
            sent(halo(first + step))
        return carry

    lax.fori_loop(0, ITERS, iteration, 0)


def per_device(axes, start, tiles, tile_cols):
    NZ, NX, NY = axes
    NQ = NX * NY
    rows_a, rows_b = TILE // NQ, 2 * TILE // NQ
    dma = pltpu.SemaphoreType.DMA
    steps = ITERS * DEGREE

    def vmem(*shape, dtype=F32):
        return pltpu.VMEM(shape, dtype)

    last_y, last_w = pl.pallas_call(
        functools.partial(kernel, axes),
        out_shape=(jax.ShapeDtypeStruct((OWN, TILE), F32), jax.ShapeDtypeStruct((TILE, TILE), F32)),
        in_specs=[pl.BlockSpec(memory_space=pltpu.HBM)] * 3,
        out_specs=(ANY, ANY),
        scratch_shapes=[
            pltpu.SMEM((BR * TPR,), jnp.int32),
            vmem(BR * TPR, TILE, TILE, dtype=BF16),
            vmem(2, OWN, EXT, dtype=BF16),
            vmem(OWN, TILE),
            vmem(steps, EXT, TILE, dtype=BF16),
            vmem(OWN, TILE), vmem(OWN, TILE), vmem(ITERS, EXT, TILE), vmem(ITERS, EXT, TILE),
            vmem(TILE, TILE), vmem(ITERS, TILE, TILE), vmem(ITERS, TILE, TILE), vmem(TILE, TILE), vmem(EXT, TILE),
            vmem(ITERS, NQ, rows_a, TILE), vmem(ITERS, NQ, rows_b, TILE),
            vmem(ITERS, NQ, rows_a, TILE), vmem(ITERS, NQ, rows_b, TILE),
            vmem(ITERS, NZ, rows_a, TILE), vmem(ITERS, NZ, rows_b, TILE),
            vmem(ITERS, NQ, rows_a, TILE), vmem(ITERS, NQ, rows_b, TILE),
            dma((3,)), dma((2,)), dma((steps, 2)), dma((steps, 2)), dma((ITERS, 2)), dma((ITERS, 2)),
            dma((2,)), dma((2,)), dma((2,)), dma((2,)),
        ] + [dma((ITERS,))] * 6,
        compiler_params=pltpu.CompilerParams(
            collective_id=0, has_side_effects=True, vmem_limit_bytes=24 * 2**20
        ),
        name="embed",
    )(*[pltpu.with_memory_space_constraint(a, pltpu.HBM) for a in (tile_cols, start, tiles)])
    return dot(last_y, last_w, ((1,), (1,)), HIGHEST)


def solution(mesh, axes=AXES):
    placed = (P("rows", "cols"), P("rows", None, None), P("rows"))
    return jax.shard_map(
        functools.partial(per_device, axes),
        mesh=mesh, in_specs=placed, out_specs=P("rows", "cols"), check_vma=False,
    )
```
